32 devices in a mesh: dp: 32 (over z, y, x, core).
Axes of the slice: x: 2, y: 2, z: 4, core: 2. Of those that a mesh axis runs over, the one named last changes fastest.
Arguments:
- byte_inputs: bfloat16 [64, 2048, 768], P('dp'), may hold values from -6 to 6
- lengths: int32 [64], P('dp'), may hold values from 512 to 2048, as said below
- key_mask: int32 [64, 2048], P('dp'), may hold values from 0 to 1, as said below
- latents_cot: bfloat16 [64, 256, 1280], P('dp'), may hold values from -6 to 6
- latent_array: bfloat16 [256, 1280], P('dp'), may hold values from -6 to 6
- lat_gain: bfloat16 [1280], P('dp'), may hold values from 0.099609375 to 1.8984375
- query_weight: bfloat16 [1280, 768], P('dp'), may hold values from -0.3125 to 0.3125
- in_gain: bfloat16 [768], P('dp'), may hold values from 0.099609375 to 1.8984375
- key_weight: bfloat16 [768, 768], P('dp'), may hold values from -0.21875 to 0.21875
- value_weight: bfloat16 [768, 768], P('dp'), may hold values from -0.21875 to 0.21875
- out_weight: bfloat16 [768, 1280], P('dp'), may hold values from -1.75 to 1.75
- mlp_gain: bfloat16 [1280], P('dp'), may hold values from 0.099609375 to 1.8984375
- mlp_in_weight: bfloat16 [1280, 1280], P('dp'), may hold values from -0.15625 to 0.15625
- mlp_out_weight: bfloat16 [1280, 1280], P('dp'), may hold values from -0.15625 to 0.15625
Outputs:
- latents: bfloat16 [64, 256, 1280], P('dp')
- inputs_grad: bfloat16 [64, 2048, 768], P('dp')
- latent_array_grad: float32 [256, 1280], P('dp')
- lat_gain_grad: float32 [1280], P('dp')
- query_weight_grad: float32 [1280, 768], P('dp')
- in_gain_grad: float32 [768], P('dp')
- key_weight_grad: float32 [768, 768], P('dp')
- value_weight_grad: float32 [768, 768], P('dp')
- out_weight_grad: float32 [768, 1280], P('dp')
- mlp_gain_grad: float32 [1280], P('dp')
- mlp_in_weight_grad: float32 [1280, 1280], P('dp')
- mlp_out_weight_grad: float32 [1280, 1280], P('dp')
The draws below stay inside these ranges and needn't reach their ends.
Inputs may be any that keep to these rules, and one draw needn't show every extreme that they name: `lengths`: sequence 0 has 2048 used slots; every other has 512, 1024 or 2048. `key_mask`: slot 0 of every sequence is 1.
All inputs are finite; a program needn't handle non-finite values.
Results may differ from the reference program's by a relative error of at most 0.014.
The reference program's roundings to bfloat16 on the way count: a program that leaves them out, or rounds other values in their place, can miss the bound.
Values may be sent and summed in bfloat16 or wider, within the bound.
No kernel may reach another device: no remote copies, remote signals or barrier semaphores. Data moves between devices by JAX's collectives and lax.ppermute only.
A program may use at most 320 MiB of HBM per device.

```python
import math
import jax
import jax.numpy as jnp
from jax import lax

DL = 1280
DI = 768
NLAT = 256
HEADS = 8
LEN = 2048
SEQS = 64


def draw_lengths(key, part):
    levels = jax.random.randint(key, (SEQS,), 0, 3)
    table = jnp.array([LEN // 4, LEN // 2, LEN], dtype=jnp.int32)
    picked = jnp.sum(jnp.where(levels[:, None] == jnp.arange(3)[None, :], table[None, :], 0), axis=1)
    places = jnp.arange(SEQS)
    return jnp.where(places == 0, LEN, picked).astype(jnp.int32)


def draw_key_mask(key, part):
    digits = jax.random.randint(key, (SEQS, LEN), 0, 10)
    ones = jnp.where(digits != 0, 1, 0)
    first = jnp.arange(LEN)[None, :] == 0
    return jnp.where(first, 1, ones).astype(jnp.int32)


def raised(drawn, stream_key, source, target, blocks, factor):
    owner, partner = [(jnp.arange(drawn.shape[dim]) // (drawn.shape[dim] // blocks)).reshape([-1 if axis == dim else 1 for axis in range(drawn.ndim)]) for dim in (source, target)]
    chosen = jax.random.permutation(stream_key, blocks)[partner]
    strong = (owner == chosen) | (owner == (partner + blocks // 2) % blocks)
    return jnp.where(strong, factor * drawn, drawn)


def level_of(rng, extent, split, low, largest):
    factor_of = 1.0
    for axis_at, blocks in split:
        steps = jax.random.uniform(jax.random.fold_in(jax.random.fold_in(rng, 6), axis_at), (blocks,), jnp.float32, low / len(split), largest / len(split))
        factor_of = factor_of * jnp.repeat(jnp.exp(steps), extent[axis_at] // blocks).reshape((-1,) + (1,) * (len(extent) - 1 - axis_at))
    return factor_of


def normal_values(rng, shape, scale, reach, split=(), held_as=jnp.bfloat16):
    factor_of = level_of(rng, shape, split, -0.22, 0.18) if split else 1.0
    entries = jax.random.normal(rng, shape, jnp.float32) * scale * factor_of
    return jnp.minimum(jnp.maximum(entries, -reach), reach).astype(held_as)


def heavy_noise(own_key, shape, width, most, cuts, heavy, kind=jnp.bfloat16):
    values = width * jax.random.normal(own_key, shape, jnp.float32)
    if cuts:
        values = values * level_of(own_key, shape, cuts, -0.22, 0.18)
    return jnp.clip(raised(values, jax.random.fold_in(own_key, 3), *heavy), -most, most).astype(kind)


def setup_inputs(seed: int = 0) -> dict:
    streams_of = jax.random.split(jax.random.key(seed), 15)
    byte_inputs = heavy_noise(streams_of[0], (SEQS, LEN, DI), 1.0, 6.0, ((0, 32),), (0, 2, 32, 2.75))
    lengths = draw_lengths(jax.random.fold_in(streams_of[14], 71), 0)
    key_mask = draw_key_mask(jax.random.fold_in(streams_of[14], 71), 0)
    latents_cot = heavy_noise(streams_of[3], (SEQS, NLAT, DL), 1.0, 6.0, ((0, 32),), (0, 1, 32, 2.75))
    latent_array = normal_values(streams_of[4], (NLAT, DL), 1.0, 6.0, ((0, 32),))
    lat_gain = jnp.clip(1.0 + 0.18 * jax.random.normal(streams_of[5], (DL,), jnp.float32), 0.099609375, 1.8984375).astype(jnp.bfloat16)
    query_weight = normal_values(streams_of[6], (DL, DI), (DL // 4) ** -0.5, 0.3125, ((0, 32),))
    in_gain = jnp.clip(1.0 + 0.18 * jax.random.normal(streams_of[7], (DI,), jnp.float32), 0.099609375, 1.8984375).astype(jnp.bfloat16)
    key_weight = normal_values(streams_of[8], (DI, DI), DI ** -0.5, 0.21875, ((0, 32),))
    value_weight = normal_values(streams_of[9], (DI, DI), DI ** -0.5, 0.21875, ((0, 32),))
    out_weight = normal_values(streams_of[10], (DI, DL), (DI // 64) ** -0.5, 1.75, ((0, 32),))
    mlp_gain = jnp.clip(1.0 + 0.18 * jax.random.normal(streams_of[11], (DL,), jnp.float32), 0.099609375, 1.8984375).astype(jnp.bfloat16)
    mlp_in_weight = normal_values(streams_of[12], (DL, DL), DL ** -0.5, 0.15625, ((0, 32),))
    mlp_out_weight = normal_values(streams_of[13], (DL, DL), DL ** -0.5, 0.15625, ((0, 32),))
    return {"byte_inputs": byte_inputs, "lengths": lengths, "key_mask": key_mask, "latents_cot": latents_cot, "latent_array": latent_array, "lat_gain": lat_gain, "query_weight": query_weight, "in_gain": in_gain, "key_weight": key_weight, "value_weight": value_weight, "out_weight": out_weight, "mlp_gain": mlp_gain, "mlp_in_weight": mlp_in_weight, "mlp_out_weight": mlp_out_weight}


@jax.custom_vjp
def lower_precision(v):
    return lax.optimization_barrier(v.astype(jnp.bfloat16)).astype(jnp.float32)

@jax.custom_vjp
def lower_precision_backward(v):
    return v

def low_keep(v):
    return (lower_precision(v), None)

def low_pass(kept, grad):
    return (grad,)

def back_keep(v):
    return (v, None)

def back_low(kept, grad):
    return (lower_precision(grad),)
lower_precision.defvjp(low_keep, low_pass)
lower_precision_backward.defvjp(back_keep, back_low)
HIGH_PRECISION = lax.Precision.HIGHEST

def normed(x, gain):
    centred = x - lax.optimization_barrier(jnp.mean(x, axis=-1, keepdims=True))
    inv = lax.rsqrt(lax.optimization_barrier(jnp.mean(centred * centred, axis=-1, keepdims=True)) + 1e-05)
    return centred * inv * gain

def forward(params, inputs, valid):
    base, g_lat, w_query, g_in, key_projection, value_projection, w_out, g_mlp, w_in, w_back = params
    group = inputs.shape[0]
    head_dim = DI // HEADS
    lat_b = lower_precision(normed(base, g_lat))
    query = lower_precision(jnp.dot(lat_b, w_query, precision=HIGH_PRECISION))
    input_normed_bf = lower_precision(normed(inputs, g_in))
    key_rows = lower_precision_backward(lower_precision(jnp.einsum('wrc,ca->wra', input_normed_bf, key_projection, precision=HIGH_PRECISION)))
    value_rows = lower_precision_backward(lower_precision(jnp.einsum('wrc,ca->wra', input_normed_bf, value_projection, precision=HIGH_PRECISION)))
    queries = lower_precision_backward(jnp.broadcast_to(query, (group, NLAT, DI)))
    qh = queries.reshape(group, NLAT, HEADS, head_dim)
    kh = key_rows.reshape(group, LEN, HEADS, head_dim)
    vh = value_rows.reshape(group, LEN, HEADS, head_dim)
    raw = jnp.einsum('sihe,sjhe->shij', qh, kh, precision=HIGH_PRECISION) * (1.0 / math.sqrt(head_dim))
    scores = lower_precision_backward(jnp.where(valid[:, None, None, :], raw, -1e+30))
    probs = lower_precision(jax.nn.softmax(scores, axis=-1))
    mixed = jnp.einsum('shij,sjhe->sihe', probs, vh, precision=HIGH_PRECISION).reshape(group, NLAT, DI)
    mixed = lower_precision_backward(lower_precision(mixed))
    attn = lower_precision_backward(jnp.einsum('sie,ef->sif', mixed, w_out, precision=HIGH_PRECISION))
    x1 = base[None] + attn
    mlp_b = lower_precision(normed(x1, g_mlp))
    pre = lower_precision_backward(jnp.einsum('sid,dh->sih', mlp_b, w_in, precision=HIGH_PRECISION))
    act = lower_precision(jax.nn.gelu(pre, approximate=False))
    return x1 + jnp.einsum('sih,hf->sif', act, w_back, precision=HIGH_PRECISION)

def reference(byte_inputs, lengths, key_mask, latents_cot, latent_array, lat_gain, query_weight, in_gain, key_weight, value_weight, out_weight, mlp_gain, mlp_in_weight, mlp_out_weight):
    params = tuple((p.astype(jnp.float32) for p in (latent_array, lat_gain, query_weight, in_gain, key_weight, value_weight, out_weight, mlp_gain, mlp_in_weight, mlp_out_weight)))
    positions = jnp.arange(LEN, dtype=jnp.int32)
    valid = (positions[None, :] < lengths[:, None]) & (key_mask == 1)
    groups = SEQS // 2
    inputs_g = byte_inputs.astype(jnp.float32).reshape(groups, 2, LEN, DI)
    valid_g = valid.reshape(groups, 2, LEN)
    cot_g = latents_cot.astype(jnp.float32).reshape(groups, 2, NLAT, DL)

    def step(totals, item):
        inputs, mask_now, cot = item
        out, pull = jax.vjp(lambda p, x: forward(p, x, mask_now), params, inputs)
        grad_params, grad_inputs = pull(cot)
        totals = jax.tree.map(lambda a, b: a + b, totals, grad_params)
        return (totals, (out.astype(jnp.bfloat16), grad_inputs.astype(jnp.bfloat16)))
    zeros = jax.tree.map(jnp.zeros_like, params)
    totals, (outs, grads) = lax.scan(step, zeros, (inputs_g, valid_g, cot_g))
    latents = outs.reshape(SEQS, NLAT, DL)
    inputs_grad = grads.reshape(SEQS, LEN, DI)
    return (latents, inputs_grad, totals[0], totals[1], totals[2], totals[3], totals[4], totals[5], totals[6], totals[7], totals[8], totals[9])
```

```python
import functools
import math

import jax
import jax.numpy as jnp
from jax import lax
from jax.experimental import pallas as pl
from jax.experimental.pallas import tpu as pltpu
from jax.sharding import PartitionSpec as P

HEADS = 8
HEAD = 96
PADDED = 112
MASKED = -1e30
VMEM = 56 * 1024 * 1024
F32 = jnp.float32
BF16 = jnp.bfloat16


def nn(a, b):
    return lax.dot_general(a, b, (((1,), (0,)), ((), ())), preferred_element_type=F32)


def nt(a, b):
    return lax.dot_general(a, b, (((1,), (1,)), ((), ())), preferred_element_type=F32)


def tn(a, b):
    return lax.dot_general(a, b, (((0,), (0,)), ((), ())), preferred_element_type=F32)


def unit_rows(rows):
    centred = rows - jnp.mean(rows, axis=-1, keepdims=True)
    inverse = lax.rsqrt(jnp.mean(centred * centred, axis=-1, keepdims=True) + 1e-05)
    return centred * inverse, inverse


def norm_back(upstream, unit, inverse, gain):
    scaled = upstream * gain
    inner = (
        scaled
        - jnp.mean(scaled, axis=-1, keepdims=True)
        - unit * jnp.mean(scaled * unit, axis=-1, keepdims=True)
    )
    return inverse * inner


def gelu_slope(value_rows):
    cdf = 0.5 * (1.0 + jax.scipy.special.erf(value_rows * (1.0 / math.sqrt(2.0))))
    return cdf + value_rows * jnp.exp(-0.5 * value_rows * value_rows) * (
        1.0 / math.sqrt(2.0 * math.pi)
    )


def grid_of(devices):
    known = {32: (4, 2, 2, 2), 128: (4, 4, 4, 2)}
    if devices in known:
        return known[devices]
    dims, left = [], devices
    while left > 1:
        step = next(f for f in (2, 3, 4, 5, 7, left) if left % f == 0)
        dims.insert(0, step)
        left //= step
    return tuple(dims)


class Grid:
    def __init__(self, devices):
        self.devices = devices
        self.dims = grid_of(devices)
        self.strides = tuple(math.prod(self.dims[i + 1 :]) for i in range(len(self.dims)))
        me = lax.axis_index("dp")
        self.mine = tuple((me // s) % k for s, k in zip(self.strides, self.dims))
        last = len(self.dims) - 1
        near = list(range(1, last))
        self.order_a = (0, *near[::-1], last) if last else (0,)
        self.order_b = (0, *near, last) if last else (0,)

    def shift(self, dim, r):
        k, s = self.dims[dim], self.strides[dim]
        pairs = []
        for i in range(self.devices):
            at = (i // s) % k
            pairs.append((i, i + (((at + r) % k) - at) * s))
        return pairs

    def gather(self, block, order):
        stack = block[None]
        for dim in order:
            k = self.dims[dim]
            parts = [stack]
            for r in range(1, k):
                parts.append(lax.ppermute(stack, "dp", self.shift(dim, k - r)))
            stack = jnp.concatenate(parts, axis=0)
        return stack

    def found(self, order):
        sizes = [self.dims[dim] for dim in order]
        index = jnp.zeros((1,) * len(self.dims), jnp.int32)
        for n, dim in enumerate(order):
            step = math.prod(sizes[:n])
            away = (jnp.arange(self.dims[dim], dtype=jnp.int32) - self.mine[dim]) % self.dims[dim]
            shape = [1] * len(self.dims)
            shape[dim] = self.dims[dim]
            index = index + (away * step).reshape(shape)
        return index.reshape(-1)

    def scatter_sum(self, whole, order):
        rest = list(range(len(self.dims)))
        wire = whole.dtype
        value = whole.reshape(*self.dims, *whole.shape[1:])
        for dim in order:
            axis = rest.index(dim)
            k, me = self.dims[dim], self.mine[dim]

            def take(at):
                return lax.dynamic_index_in_dim(value, at, axis, keepdims=False)

            total = take(me).astype(F32)
            for r in range(1, k):
                sent = take((me + r) % k)
                total = total + lax.ppermute(sent, "dp", self.shift(dim, r)).astype(F32)
            rest.pop(axis)
            value = total if not rest else total.astype(wire)
        return value


def prepare_kernel(
    cuts, place_ref, a_ref, b_ref, wt_ref, wq_ref, lat_ref, q_ref, qt_ref, gin_ref, glat_ref, gmlp_ref, kv_ref
):
    devices, width = a_ref.shape[0], a_ref.shape[2]
    k_rows, q_top, q_low, l_rows, l_width = cuts
    q_rows = q_top + q_low
    lines = []
    for d in range(devices):
        a = a_ref.at[place_ref[0, d]]
        b = b_ref.at[place_ref[1, d]]
        kv_ref[d * k_rows : (d + 1) * k_rows, :width] = a[:k_rows]
        kv_ref[d * k_rows : (d + 1) * k_rows, width:] = b[:k_rows]
        wq_ref[d * q_rows : d * q_rows + q_top] = a[k_rows : k_rows + q_top]
        at = k_rows + q_low
        wq_ref[d * q_rows + q_top : (d + 1) * q_rows] = b[k_rows:at]
        lat_ref[d * l_rows : (d + 1) * l_rows, :width] = b[at : at + l_rows]
        spare = b[at + l_rows : at + 2 * l_rows]
        lat_ref[d * l_rows : (d + 1) * l_rows, width:] = spare[:, : l_width - width]
        lines.append(spare[:1, l_width - width :].astype(F32))
    first = 0
    for ref, size in ((gin_ref, k_rows), (glat_ref, q_rows), (gmlp_ref, q_rows)):
        ref[...] = jnp.concatenate([line[:, first : first + size] for line in lines], axis=1)
        first += size
    for c in range(0, wt_ref.shape[0], width):
        wt_ref[c : c + width] = kv_ref[:, c : c + width].T
    unit, _ = unit_rows(lat_ref[...].astype(F32))
    query = nn((unit * glat_ref[...]).astype(BF16), wq_ref[...])
    qt_ref[...] = query.T.astype(BF16)
    query = query.astype(BF16)
    column = lax.broadcasted_iota(jnp.int32, (query.shape[0], PADDED - HEAD), 1)
    ones = jnp.where(column == 0, 1.0, 0.0).astype(BF16)
    for h in range(HEADS):
        q_ref[h] = jnp.concatenate([query[:, h * HEAD : (h + 1) * HEAD], ones], axis=1)


def prepare(stack_a, stack_b, places, cuts):
    devices, _, width = stack_a.shape
    k_rows, q_top, q_low, l_rows, l_width = cuts
    rows = devices * l_rows
    vmem = pl.BlockSpec(memory_space=pltpu.VMEM)
    shapes = [
        ((2 * width, width), BF16),
        ((devices * (q_top + q_low), width), BF16),
        ((rows, l_width), BF16),
        ((HEADS, rows, PADDED), BF16),
        ((width, rows), BF16),
        ((1, width), F32),
        ((1, l_width), F32),
        ((1, l_width), F32),
    ]
    return pl.pallas_call(
        functools.partial(prepare_kernel, cuts),
        in_specs=[pl.BlockSpec(memory_space=pltpu.SMEM), vmem, vmem],
        out_specs=[vmem] * len(shapes),
        out_shape=[jax.ShapeDtypeStruct(*s) for s in shapes],
        scratch_shapes=[pltpu.VMEM((width, 2 * width), BF16)],
        compiler_params=pltpu.CompilerParams(vmem_limit_bytes=VMEM),
        name="prepare",
    )(places, stack_a, stack_b)


def project_kernel(x_ref, gain_ref, w_ref, addend_ref, normed_ref, k_ref, v_ref):
    unit, _ = unit_rows(x_ref[0].astype(F32))
    normed = (unit * gain_ref[...]).astype(BF16)
    normed_ref[0] = normed
    slots = normed.shape[0]
    both = nt(w_ref[...], normed).astype(BF16)
    row = lax.broadcasted_iota(jnp.int32, (PADDED - HEAD, slots), 0)
    mask_rows = jnp.where(row == 0, jnp.broadcast_to(addend_ref[0], row.shape), 0.0).astype(BF16)
    one_rows = jnp.where(row < 3, 1.0, 0.0).astype(BF16)
    for h in range(HEADS):
        k_ref[0, h, :HEAD] = both[h * HEAD : (h + 1) * HEAD]
        k_ref[0, h, HEAD:] = mask_rows
        v_ref[0, h, :HEAD] = both[(HEADS + h) * HEAD : (HEADS + h + 1) * HEAD]
        v_ref[0, h, HEAD:] = one_rows


def project(x, gain, weights, addend, tile=512):
    seqs, slots, width = x.shape
    rows = pl.BlockSpec((1, tile, width), lambda s, j: (s, j, 0))
    heads = pl.BlockSpec((1, HEADS, PADDED, tile), lambda s, j: (s, 0, 0, j))
    whole = lambda a: pl.BlockSpec(a.shape, lambda s, j: (0,) * a.ndim)
    return pl.pallas_call(
        project_kernel,
        grid=(seqs, slots // tile),
        in_specs=[rows, whole(gain), whole(weights), pl.BlockSpec((1, 1, tile), lambda s, j: (s, 0, j))],
        out_specs=[rows, heads, heads],
        out_shape=[
            jax.ShapeDtypeStruct(x.shape, BF16),
            jax.ShapeDtypeStruct((seqs, HEADS, PADDED, slots), BF16),
            jax.ShapeDtypeStruct((seqs, HEADS, PADDED, slots), BF16),
        ],
        compiler_params=pltpu.CompilerParams(vmem_limit_bytes=VMEM),
        cost_estimate=pl.CostEstimate(
            flops=4 * seqs * slots * width * width, bytes_accessed=10 * seqs * slots * width, transcendentals=0
        ),
        name="project",
    )(x, gain, weights, addend)


def attend_kernel(chunk, scale, q_ref, k_ref, v_ref, mixed_ref, log_ref, score_ref):
    slots = k_ref.shape[-1]
    outs, logs = [], []
    for h in range(q_ref.shape[0]):
        score = score_ref.at[h % 2]
        top = None
        for j in range(0, slots, chunk):
            piece = nn(q_ref[h], k_ref[0, h, :, j : j + chunk])
            score[:, j : j + chunk] = piece
            for t in range(0, chunk, 128):
                part = piece[:, t : t + 128]
                top = part if top is None else jnp.maximum(top, part)
        top = jnp.max(top, axis=-1, keepdims=True)
        total = None
        for j in range(0, slots, chunk):
            power = jnp.exp2((score[:, j : j + chunk] - top) * scale).astype(BF16)
            piece = nt(power, v_ref[0, h, :, j : j + chunk])
            total = piece if total is None else total + piece
        weight = total[:, HEAD : HEAD + 1]
        outs.append(total[:, :HEAD] / weight)
        logs.append(top * scale + jnp.log2(weight))
    mixed_ref[0] = jnp.concatenate(outs, axis=1)
    for h, log in enumerate(logs):
        log_ref[0, h] = jnp.broadcast_to(log, log_ref.shape[2:])


def attend(q, k, v, chunk=1024, group=4):
    seqs, _, _, slots = k.shape
    rows = q.shape[1]
    scale = math.log2(math.e) / math.sqrt(HEAD)
    heads = pl.BlockSpec((1, group, PADDED, slots), lambda s, g: (s, g, 0, 0))
    return pl.pallas_call(
        functools.partial(attend_kernel, chunk, scale),
        grid=(seqs, HEADS // group),
        in_specs=[pl.BlockSpec((group, rows, PADDED), lambda s, g: (g, 0, 0)), heads, heads],
        out_specs=[
            pl.BlockSpec((1, rows, group * HEAD), lambda s, g: (s, 0, g)),
            pl.BlockSpec((1, group, rows, 128), lambda s, g: (s, g, 0, 0)),
        ],
        out_shape=[
            jax.ShapeDtypeStruct((seqs, rows, HEADS * HEAD), F32),
            jax.ShapeDtypeStruct((seqs, HEADS, rows, 128), F32),
        ],
        scratch_shapes=[pltpu.VMEM((2, rows, slots), F32)],
        compiler_params=pltpu.CompilerParams(vmem_limit_bytes=VMEM),
        cost_estimate=pl.CostEstimate(
            flops=16 * seqs * rows * slots * HEADS * HEAD,
            bytes_accessed=4 * seqs * HEADS * PADDED * slots,
            transcendentals=seqs * HEADS * rows * slots,
        ),
        name="attend",
    )(q, k, v)


def attend_back_kernel(
    chunk, scale, factor, q_ref, qt_ref, k_ref, v_ref, log_ref, dm_ref, dmt_ref, dq_ref, dk_ref, dv_ref
):
    slots = k_ref.shape[-1]
    grads = []
    for h in range(q_ref.shape[0]):
        log = log_ref[0, h][:, :1]
        mine = slice(h * HEAD, (h + 1) * HEAD)
        total = None
        for j in range(0, slots, chunk):
            keys = k_ref[0, h, :, j : j + chunk]
            probs = jnp.exp2(nn(q_ref[h], keys) * scale - log)
            less = nn(dm_ref[0, h], v_ref[0, h, :, j : j + chunk])
            d_scores = (probs * less).astype(BF16)
            dv_ref[0, mine, j : j + chunk] = nn(dmt_ref[0, mine], probs.astype(BF16)).astype(BF16)
            dk_ref[0, mine, j : j + chunk] = (nn(qt_ref[mine], d_scores) * factor).astype(BF16)
            piece = nt(d_scores, keys[:HEAD])
            total = piece if total is None else total + piece
        grads.append((total * factor).astype(BF16))
    dq_ref[0] = jnp.concatenate(grads, axis=1)


def attend_back(q, qt, k, v, log, dm, dmt, chunk=2048, group=4):
    seqs, _, _, slots = k.shape
    rows = q.shape[1]
    scale = math.log2(math.e) / math.sqrt(HEAD)
    heads = pl.BlockSpec((1, group, PADDED, slots), lambda s, g: (s, g, 0, 0))
    features = pl.BlockSpec((1, group * HEAD, slots), lambda s, g: (s, g, 0))
    return pl.pallas_call(
        functools.partial(attend_back_kernel, chunk, scale, 1.0 / math.sqrt(HEAD)),
        grid=(seqs, HEADS // group),
        in_specs=[
            pl.BlockSpec((group, rows, PADDED), lambda s, g: (g, 0, 0)),
            pl.BlockSpec((group * HEAD, rows), lambda s, g: (g, 0)),
            heads,
            heads,
            pl.BlockSpec((1, group, rows, 128), lambda s, g: (s, g, 0, 0)),
            pl.BlockSpec((1, group, rows, PADDED), lambda s, g: (s, g, 0, 0)),
            pl.BlockSpec((1, group * HEAD, rows), lambda s, g: (s, g, 0)),
        ],
        out_specs=[pl.BlockSpec((1, rows, group * HEAD), lambda s, g: (s, 0, g)), features, features],
        out_shape=[
            jax.ShapeDtypeStruct((seqs, rows, HEADS * HEAD), BF16),
            jax.ShapeDtypeStruct((seqs, HEADS * HEAD, slots), BF16),
            jax.ShapeDtypeStruct((seqs, HEADS * HEAD, slots), BF16),
        ],
        compiler_params=pltpu.CompilerParams(vmem_limit_bytes=VMEM),
        cost_estimate=pl.CostEstimate(
            flops=40 * seqs * rows * slots * HEADS * HEAD,
            bytes_accessed=8 * seqs * HEADS * PADDED * slots,
            transcendentals=seqs * HEADS * rows * slots,
        ),
        name="attend_back",
    )(q, qt, k, v, log, dm, dmt)


def kv_grad_kernel(dk_ref, dv_ref, normed_ref, gk_ref, gv_ref, total_ref):
    step = pl.program_id(0) * pl.num_programs(1) + pl.program_id(1)
    normed = normed_ref[0]
    for n, ref in enumerate((dk_ref, dv_ref)):
        piece = nn(ref[0], normed)

        @pl.when(step == 0)
        def _():
            total_ref[n] = piece

        @pl.when(step > 0)
        def _():
            total_ref[n] += piece

    @pl.when(step == pl.num_programs(0) * pl.num_programs(1) - 1)
    def _():
        gk_ref[...] = total_ref[0].T.astype(BF16)
        gv_ref[...] = total_ref[1].T.astype(BF16)


def kv_grad(dk, dv, normed, tile=1024):
    seqs, features, slots = dk.shape
    width = normed.shape[-1]
    columns = pl.BlockSpec((1, features, tile), lambda s, j: (s, 0, j))
    whole = pl.BlockSpec((width, features), lambda s, j: (0, 0))
    return pl.pallas_call(
        kv_grad_kernel,
        grid=(seqs, slots // tile),
        in_specs=[columns, columns, pl.BlockSpec((1, tile, width), lambda s, j: (s, j, 0))],
        out_specs=[whole, whole],
        out_shape=[jax.ShapeDtypeStruct((width, features), BF16)] * 2,
        scratch_shapes=[pltpu.VMEM((2, features, width), F32)],
        compiler_params=pltpu.CompilerParams(vmem_limit_bytes=VMEM),
        cost_estimate=pl.CostEstimate(
            flops=4 * seqs * slots * width * features, bytes_accessed=6 * seqs * slots * width, transcendentals=0
        ),
        name="kv_grad",
    )(dk, dv, normed)


def input_grad_kernel(dk_ref, dv_ref, w_ref, gain_ref, x_ref, out_ref):
    features = dk_ref.shape[1]
    upstream = tn(dk_ref[0], w_ref[:features]) + tn(dv_ref[0], w_ref[features:])
    unit, inverse = unit_rows(x_ref[0].astype(F32))
    out_ref[0] = norm_back(upstream, unit, inverse, gain_ref[...]).astype(BF16)


def input_grad(dk, dv, weights, gain, x, tile=512):
    seqs, features, slots = dk.shape
    width = x.shape[-1]
    columns = pl.BlockSpec((1, features, tile), lambda s, j: (s, 0, j))
    rows = pl.BlockSpec((1, tile, width), lambda s, j: (s, j, 0))
    whole = lambda a: pl.BlockSpec(a.shape, lambda s, j: (0,) * a.ndim)
    return pl.pallas_call(
        input_grad_kernel,
        grid=(seqs, slots // tile),
        in_specs=[columns, columns, whole(weights), whole(gain), rows],
        out_specs=rows,
        out_shape=jax.ShapeDtypeStruct(x.shape, BF16),
        compiler_params=pltpu.CompilerParams(vmem_limit_bytes=VMEM),
        cost_estimate=pl.CostEstimate(
            flops=4 * seqs * slots * width * features, bytes_accessed=8 * seqs * slots * width, transcendentals=0
        ),
        name="input_grad",
    )(dk, dv, weights, gain, x)


def local(
    byte_inputs,
    lengths,
    key_mask,
    latents_cot,
    latent_array,
    lat_gain,
    query_weight,
    in_gain,
    key_weight,
    value_weight,
    out_weight,
    mlp_gain,
    mlp_in_weight,
    mlp_out_weight,
):
    devices = lax.axis_size("dp")
    grid = Grid(devices)
    seqs, length, width = byte_inputs.shape
    k_rows, q_rows, l_rows = key_weight.shape[0], query_weight.shape[0], latent_array.shape[0]
    l_width = latent_array.shape[1]
    rows = devices * l_rows
    q_top = k_rows if q_rows > k_rows else q_rows // 2
    q_low = q_rows - q_top
    cuts = (k_rows, q_top, q_low, l_rows, l_width)

    late = lax.all_gather(jnp.concatenate([out_weight, mlp_in_weight, mlp_out_weight], axis=0), "dp")

    gains = jnp.concatenate([in_gain, lat_gain, mlp_gain])
    spare = 2 * width - l_width
    gain_rows = jnp.broadcast_to(jnp.pad(gains, (0, spare - gains.shape[0])), (l_rows, spare))
    block_a = jnp.concatenate([key_weight, query_weight[:q_top]], axis=0)
    block_b = jnp.concatenate(
        [
            value_weight,
            query_weight[q_top:],
            latent_array[:, :width],
            jnp.concatenate([latent_array[:, width:], gain_rows], axis=1),
        ],
        axis=0,
    )
    stack_a = grid.gather(block_a, grid.order_a)
    stack_b = grid.gather(block_b, grid.order_b)
    places = jnp.stack([grid.found(grid.order_a), grid.found(grid.order_b)])
    kv_weights, w_query, base, q, qt, g_in, g_lat, g_mlp = prepare(stack_a, stack_b, places, cuts)

    positions = jnp.arange(length, dtype=jnp.int32)
    valid = (positions[None, :] < lengths[:, None]) & (key_mask == 1)
    addend = jnp.where(valid, 0.0, MASKED).astype(F32)[:, None]
    normed, k, v = project(byte_inputs, g_in, kv_weights, addend)
    mixed32, log = attend(q, k, v)

    w_out = late[:, :k_rows].reshape(-1, l_width)
    w_in = late[:, k_rows : k_rows + q_rows].reshape(-1, l_width)
    w_back = late[:, k_rows + q_rows :].reshape(-1, l_width)
    base32 = base.astype(F32)
    lat_unit, lat_inv = unit_rows(base32)
    lat_b = (lat_unit * g_lat).astype(BF16)
    mixed = mixed32.astype(BF16)
    x_one = base32[None] + jnp.einsum("sie,ef->sif", mixed, w_out, preferred_element_type=F32)
    mlp_unit, mlp_inv = unit_rows(x_one)
    mlp_b = (mlp_unit * g_mlp).astype(BF16)
    pre = jnp.einsum("sid,dh->sih", mlp_b, w_in, preferred_element_type=F32)
    act = jax.nn.gelu(pre, approximate=False).astype(BF16)
    latents = (
        x_one + jnp.einsum("sih,hf->sif", act, w_back, preferred_element_type=F32)
    ).astype(BF16)

    cot32 = latents_cot.astype(F32)
    d_act = jnp.einsum("sif,hf->sih", latents_cot, w_back, preferred_element_type=F32)
    d_pre = (d_act * gelu_slope(pre)).astype(BF16)
    d_mlpnorm = jnp.einsum("sih,dh->sid", d_pre, w_in, preferred_element_type=F32)
    d_x_one = cot32 + norm_back(d_mlpnorm, mlp_unit, mlp_inv, g_mlp)
    d_attn = d_x_one.astype(BF16)
    d_mixed = jnp.einsum("sif,ef->sie", d_attn, w_out, preferred_element_type=F32).astype(BF16)
    grad_back = jnp.einsum("sih,sif->hf", act, latents_cot, preferred_element_type=F32)
    grad_in = jnp.einsum("sid,sih->dh", mlp_b, d_pre, preferred_element_type=F32)
    grad_out = jnp.einsum("sie,sif->ef", mixed, d_attn, preferred_element_type=F32)

    def blocks(g):
        return g.astype(BF16).reshape(devices, g.shape[0] // devices, g.shape[1])

    back_order_a, back_order_b = grid.order_a[::-1], grid.order_b[::-1]
    in_grad = grid.scatter_sum(blocks(grad_in), back_order_a)
    back_grad = grid.scatter_sum(blocks(grad_back), back_order_b)
    out_grad = lax.psum_scatter(grad_out, "dp", scatter_dimension=0, tiled=True)

    dm_heads = d_mixed.reshape(seqs, rows, HEADS, HEAD).transpose(0, 2, 1, 3)
    mixed_heads = mixed32.reshape(seqs, rows, HEADS, HEAD).transpose(0, 2, 1, 3)
    centre = -jnp.sum(dm_heads.astype(F32) * mixed_heads, axis=-1, keepdims=True)
    high = lax.reduce_precision(centre, 8, 7)
    middle = lax.reduce_precision(centre - high, 8, 7)
    low = centre - high - middle
    pieces = [dm_heads] + [p.astype(BF16) for p in (high, middle, low)]
    pieces.append(jnp.zeros((seqs, HEADS, rows, PADDED - HEAD - 3), BF16))
    dm = jnp.concatenate(pieces, axis=-1)
    d_query, dk, dv = attend_back(q, qt, k, v, log, dm, d_mixed.transpose(0, 2, 1))

    grad_query = jnp.einsum("ic,sia->ca", lat_b, d_query, preferred_element_type=F32)
    d_latnorm = jnp.einsum("sia,ca->ic", d_query, w_query, preferred_element_type=F32)
    base_local = norm_back(d_latnorm, lat_unit, lat_inv, g_lat) + jnp.sum(d_x_one, axis=0)
    query_blocks, base_blocks = blocks(grad_query), blocks(base_local)
    room = jnp.zeros((devices, l_rows, spare), BF16)
    sum_a = grid.scatter_sum(query_blocks[:, :q_top], back_order_a)
    sum_b = grid.scatter_sum(
        jnp.concatenate(
            [
                query_blocks[:, q_top:],
                base_blocks[:, :, :width],
                jnp.concatenate([base_blocks[:, :, width:], room], axis=2),
            ],
            axis=1,
        ),
        back_order_b,
    )
    query_grad = jnp.concatenate([sum_a, sum_b[:q_low]], axis=0)
    base_grad = jnp.concatenate(
        [sum_b[q_low : q_low + l_rows], sum_b[q_low + l_rows :, : l_width - width]], axis=1
    )

    grad_key, grad_value = kv_grad(dk, dv, normed)
    key_grad = grid.scatter_sum(blocks(grad_key), back_order_a)
    value_grad = grid.scatter_sum(blocks(grad_value), back_order_b)
    inputs_grad = input_grad(dk, dv, kv_weights, g_in, byte_inputs)

    def gain_grad(gain, *pairs):
        total = sum(jnp.sum(g * w.astype(F32), axis=1) for g, w in pairs)
        return total / gain.astype(F32)

    gin_grad = gain_grad(in_gain, (key_grad, key_weight), (value_grad, value_weight))
    glat_grad = gain_grad(lat_gain, (query_grad, query_weight))
    gmlp_grad = gain_grad(mlp_gain, (in_grad, mlp_in_weight))
    return (
        latents,
        inputs_grad,
        base_grad,
        glat_grad,
        query_grad,
        gin_grad,
        key_grad,
        value_grad,
        out_grad,
        gmlp_grad,
        in_grad,
        back_grad,
    )


def solution(mesh):
    in_specs = (
        P("dp", None, None),
        P("dp"),
        P("dp", None),
        P("dp", None, None),
        P("dp", None),
        P("dp"),
        P("dp", None),
        P("dp"),
        P("dp", None),
        P("dp", None),
        P("dp", None),
        P("dp"),
        P("dp", None),
        P("dp", None),
    )
    out_specs = (
        P("dp", None, None),
        P("dp", None, None),
        P("dp", None),
        P("dp"),
        P("dp", None),
        P("dp"),
        P("dp", None),
        P("dp", None),
        P("dp", None),
        P("dp"),
        P("dp", None),
        P("dp", None),
    )
    return jax.shard_map(local, mesh=mesh, in_specs=in_specs, out_specs=out_specs, check_vma=False)
```

```python
import functools
import math

import jax
import jax.numpy as jnp
from jax import lax
from jax.experimental import pallas as pl
from jax.experimental.pallas import tpu as pltpu
from jax.sharding import PartitionSpec as P

HEADS = 8
HEAD = 96
PADDED = 112
MASKED = -1e30
VMEM = 56 * 1024 * 1024
F32 = jnp.float32
BF16 = jnp.bfloat16


def nn(a, b):
    return lax.dot_general(a, b, (((1,), (0,)), ((), ())), preferred_element_type=F32)


def nt(a, b):
    return lax.dot_general(a, b, (((1,), (1,)), ((), ())), preferred_element_type=F32)


def tn(a, b):
    return lax.dot_general(a, b, (((0,), (0,)), ((), ())), preferred_element_type=F32)


def unit_rows(rows):
    centred = rows - jnp.mean(rows, axis=-1, keepdims=True)
    inverse = lax.rsqrt(jnp.mean(centred * centred, axis=-1, keepdims=True) + 1e-05)
    return centred * inverse, inverse


def norm_back(upstream, unit, inverse, gain):
    scaled = upstream * gain
    inner = (
        scaled
        - jnp.mean(scaled, axis=-1, keepdims=True)
        - unit * jnp.mean(scaled * unit, axis=-1, keepdims=True)
    )
    return inverse * inner


def grid_of(devices):
    known = {32: (4, 2, 2, 2), 128: (4, 4, 4, 2)}
    if devices in known:
        return known[devices]
    dims, left = [], devices
    while left > 1:
        step = next(f for f in (2, 3, 4, 5, 7, left) if left % f == 0)
        dims.insert(0, step)
        left //= step
    return tuple(dims)


class Grid:
    def __init__(self, devices):
        self.devices = devices
        self.dims = grid_of(devices)
        self.strides = tuple(math.prod(self.dims[i + 1 :]) for i in range(len(self.dims)))
        me = lax.axis_index("dp")
        self.mine = tuple((me // s) % k for s, k in zip(self.strides, self.dims))
        last = len(self.dims) - 1
        near = list(range(1, last))
        self.order_a = (0, *near[::-1], last) if last else (0,)
        self.order_b = (0, *near, last) if last else (0,)

    def shift(self, dim, r):
        k, s = self.dims[dim], self.strides[dim]
        pairs = []
        for i in range(self.devices):
            at = (i // s) % k
            pairs.append((i, i + (((at + r) % k) - at) * s))
        return pairs

    def found(self, order):
        sizes = [self.dims[dim] for dim in order]
        index = jnp.zeros((1,) * len(self.dims), jnp.int32)
        for n, dim in enumerate(order):
            step = math.prod(sizes[:n])
            away = (jnp.arange(self.dims[dim], dtype=jnp.int32) - self.mine[dim]) % self.dims[dim]
            shape = [1] * len(self.dims)
            shape[dim] = self.dims[dim]
            index = index + (away * step).reshape(shape)
        return index.reshape(-1)


class Pair:
    def __init__(self, grid, value, cut, forward):
        self.grid, self.cut = grid, cut
        self.left = list(zip(grid.order_a, grid.order_b))
        if not forward:
            self.left.reverse()
        self.parts = [value]

    def arrange(self):
        one, other = self.left[0]
        axis = self.parts[0].ndim - 2
        if one == other:
            if len(self.parts) == 2:
                self.parts = [jnp.concatenate(self.parts, axis=axis)]
            return [one]
        if len(self.parts) == 1:
            self.parts = jnp.split(self.parts[0], [self.cut], axis=axis)
        return [one, other]


class Gather(Pair):
    def __init__(self, grid, block, cut):
        super().__init__(grid, block[None], cut, True)

    def sends(self):
        self.dims = self.arrange()
        return [[part] for part in self.parts]

    def exchange(self, sent):
        grid = self.grid
        return [
            part + [lax.ppermute(part[0], "dp", grid.shift(dim, -r)) for r in range(1, grid.dims[dim])]
            for dim, part in zip(self.dims, sent)
        ]

    def receive(self, got):
        self.left.pop(0)
        self.parts = [jnp.concatenate(part, axis=0) for part in got]


class Scatter(Pair):
    def __init__(self, grid, whole, cut):
        super().__init__(grid, whole.reshape(*grid.dims, *whole.shape[1:]), cut, False)
        self.wire = whole.dtype
        self.rest = [list(range(len(grid.dims)))] * 2

    def sends(self):
        self.dims = self.arrange()
        sent = []
        for part, dim, rest in zip(self.parts, self.dims, self.rest):
            axis, k, me = rest.index(dim), self.grid.dims[dim], self.grid.mine[dim]
            sent.append(
                [lax.dynamic_index_in_dim(part, (me + r) % k, axis, keepdims=False) for r in range(k)]
            )
        return sent

    def exchange(self, sent):
        return [
            part[:1]
            + [lax.ppermute(piece, "dp", self.grid.shift(dim, r)) for r, piece in enumerate(part) if r]
            for dim, part in zip(self.dims, sent)
        ]

    def receive(self, got):
        self.rest = [[d for d in rest if d != dim] for rest, dim in zip(self.rest, self.left.pop(0))]
        totals = [sum(piece.astype(F32) for piece in part) for part in got]
        self.parts = [total.astype(self.wire) if self.left else total for total in totals]


def overlap(jobs, work=None, *args):
    live = [job for job in jobs if job.left]
    sent, args = lax.optimization_barrier(([job.sends() for job in live], args))
    got = [job.exchange(parts) for job, parts in zip(live, sent)]
    out = work(*args) if work else ()
    got, out = lax.optimization_barrier((got, out))
    for job, parts in zip(live, got):
        job.receive(parts)
    return out


def finish(jobs):
    while any(job.left for job in jobs):
        overlap(jobs)


def prepare_kv_kernel(cuts, place_ref, stack_ref, wt_ref, gin_ref, glat_ref, gmlp_ref, kv_ref):
    devices, _, width = stack_ref.shape
    k_rows = width // devices
    lines = []
    for d in range(devices):
        mine = slice(d * k_rows, (d + 1) * k_rows)
        values = stack_ref.at[place_ref[1, d]]
        kv_ref[mine, :width] = stack_ref[place_ref[0, d], :k_rows]
        kv_ref[mine, width:] = values[k_rows : 2 * k_rows]
        lines.append(values[2 * k_rows :][:1].astype(F32))
    first = 0
    for ref, size in zip((gin_ref, glat_ref, gmlp_ref), cuts):
        ref[...] = jnp.concatenate([line[:, first : first + size] for line in lines], axis=1)
        first += size
    for c in range(0, wt_ref.shape[0], width):
        wt_ref[c : c + width] = kv_ref[:, c : c + width].T


def prepare_kv(stack, places, cuts):
    devices, _, width = stack.shape
    vmem = pl.BlockSpec(memory_space=pltpu.VMEM)
    shapes = [((2 * width, width), BF16)] + [((1, devices * size), F32) for size in cuts]
    return pl.pallas_call(
        functools.partial(prepare_kv_kernel, cuts),
        in_specs=[pl.BlockSpec(memory_space=pltpu.SMEM), vmem],
        out_specs=[vmem] * len(shapes),
        out_shape=[jax.ShapeDtypeStruct(*s) for s in shapes],
        scratch_shapes=[pltpu.VMEM((width, 2 * width), BF16)],
        compiler_params=pltpu.CompilerParams(vmem_limit_bytes=VMEM),
        cost_estimate=pl.CostEstimate(flops=0, bytes_accessed=12_000_000, transcendentals=0),
        name="prepare_kv",
    )(places, stack)


def pack_rest(query, out, latents, q_top, join):
    width = query.shape[-1]
    k_rows, l_rows, l_width = out.shape[-2], latents.shape[-2], latents.shape[-1]
    spare = 2 * width - l_width
    ends = []
    for n in range(-(-(l_width - width) // spare)):
        piece = latents[..., width + n * spare : min(width + (n + 1) * spare, l_width)]
        short = spare - piece.shape[-1]
        ends.append(join([piece, jnp.zeros((*piece.shape[:-1], short), piece.dtype)], -1) if short else piece)
    short = k_rows - len(ends) * l_rows
    if short:
        ends.append(jnp.zeros((*out.shape[:-2], short, spare), out.dtype))
    beside = join([out[..., width:], join(ends, -2)], -1)
    return join([query[..., :q_top, :], out[..., :width], beside, query[..., q_top:, :], latents[..., :width]], -2)


def unpack_rest(rows, cuts):
    q_top, q_low, k_rows, l_rows, width, l_width = cuts
    spare = 2 * width - l_width
    second = q_top + k_rows
    third = second + k_rows
    found = [
        ("query", (0, q_top), (0, width), (0, q_top), (0, width)),
        ("out", (0, k_rows), (0, width), (q_top, second), (0, width)),
        ("out", (0, k_rows), (width, l_width), (second, third), (0, l_width - width)),
        ("query", (q_top, q_top + q_low), (0, width), (third, third + q_low), (0, width)),
        ("latents", (0, l_rows), (0, width), (third + q_low, third + q_low + l_rows), (0, width)),
    ]
    for n, at in enumerate(range(width, l_width, spare)):
        end = min(at + spare, l_width)
        start = second + n * l_rows
        found.append(
            ("latents", (0, l_rows), (at, end), (start, start + l_rows), (l_width - width, l_width - width + end - at))
        )
    return found


def prepare_q_kernel(cuts, place_ref, stack_ref, glat_ref, wq_ref, wo_ref, lat_ref, q_ref, qt_ref):
    devices = stack_ref.shape[0]
    q_top, _, k_rows = cuts[:3]
    wholes = {"query": wq_ref, "out": wo_ref, "latents": lat_ref}
    for d in range(devices):
        for what, rows, columns, at, beside in unpack_rest(stack_ref.shape[1], cuts):
            ref = wholes[what]
            base = d * (ref.shape[0] // devices)
            part = 0 if at[0] < q_top + k_rows else 1
            ref[base + rows[0] : base + rows[1], columns[0] : columns[1]] = stack_ref[
                place_ref[part, d], at[0] : at[1], beside[0] : beside[1]
            ]
    unit, _ = unit_rows(lat_ref[...].astype(F32))
    query = nn((unit * glat_ref[...]).astype(BF16), wq_ref[...])
    qt_ref[...] = query.T.astype(BF16)
    query = query.astype(BF16)
    column = lax.broadcasted_iota(jnp.int32, (query.shape[0], PADDED - HEAD), 1)
    ones = jnp.where(column == 0, 1.0, 0.0).astype(BF16)
    for h in range(HEADS):
        q_ref[h] = jnp.concatenate([query[:, h * HEAD : (h + 1) * HEAD], ones], axis=1)


def prepare_q(stack, gain, places, cuts):
    devices = stack.shape[0]
    q_top, q_low, k_rows, l_rows, width, l_width = cuts
    rows = devices * l_rows
    vmem = pl.BlockSpec(memory_space=pltpu.VMEM)
    shapes = [
        (devices * (q_top + q_low), width),
        (devices * k_rows, l_width),
        (rows, l_width),
        (HEADS, rows, PADDED),
        (width, rows),
    ]
    return pl.pallas_call(
        functools.partial(prepare_q_kernel, cuts),
        in_specs=[pl.BlockSpec(memory_space=pltpu.SMEM), vmem, vmem],
        out_specs=[vmem] * len(shapes),
        out_shape=[jax.ShapeDtypeStruct(s, BF16) for s in shapes],
        compiler_params=pltpu.CompilerParams(vmem_limit_bytes=VMEM),
        cost_estimate=pl.CostEstimate(flops=0, bytes_accessed=12_000_000, transcendentals=0),
        name="prepare_q",
    )(places, stack, gain)


def project_kernel(x_ref, gain_ref, w_ref, addend_ref, normed_ref, k_ref, v_ref):
    unit, _ = unit_rows(x_ref[0].astype(F32))
    normed = (unit * gain_ref[...]).astype(BF16)
    normed_ref[0] = normed
    slots = normed.shape[0]
    both = nt(w_ref[...], normed).astype(BF16)
    row = lax.broadcasted_iota(jnp.int32, (PADDED - HEAD, slots), 0)
    mask_rows = jnp.where(row == 0, jnp.broadcast_to(addend_ref[0], row.shape), 0.0).astype(BF16)
    one_rows = jnp.where(row < 3, 1.0, 0.0).astype(BF16)
    for h in range(HEADS):
        k_ref[0, h, :HEAD] = both[h * HEAD : (h + 1) * HEAD]
        k_ref[0, h, HEAD:] = mask_rows
        v_ref[0, h, :HEAD] = both[(HEADS + h) * HEAD : (HEADS + h + 1) * HEAD]
        v_ref[0, h, HEAD:] = one_rows


def project(seq, x, gain, weights, addend, tile=512):
    _, slots, width = x.shape
    rows = pl.BlockSpec((1, tile, width), lambda j: (0, j, 0))
    heads = pl.BlockSpec((1, HEADS, PADDED, tile), lambda j: (0, 0, 0, j))
    whole = lambda a: pl.BlockSpec(a.shape, lambda j: (0,) * a.ndim)
    return pl.pallas_call(
        project_kernel,
        grid=(slots // tile,),
        in_specs=[
            pl.BlockSpec((1, tile, width), lambda j: (seq, j, 0)),
            whole(gain),
            whole(weights),
            pl.BlockSpec((1, 1, tile), lambda j: (seq, 0, j)),
        ],
        out_specs=[rows, heads, heads],
        out_shape=[
            jax.ShapeDtypeStruct((1, slots, width), BF16),
            jax.ShapeDtypeStruct((1, HEADS, PADDED, slots), BF16),
            jax.ShapeDtypeStruct((1, HEADS, PADDED, slots), BF16),
        ],
        compiler_params=pltpu.CompilerParams(vmem_limit_bytes=VMEM),
        cost_estimate=pl.CostEstimate(
            flops=8 * slots * width * width, bytes_accessed=10 * slots * width, transcendentals=0
        ),
        name="project",
    )(x, gain, weights, addend)


def attend_kernel(chunk, scale, q_ref, k_ref, v_ref, mixed_ref, log_ref, score_ref):
    slots = k_ref.shape[-1]
    outs, logs = [], []
    for h in range(q_ref.shape[0]):
        score = score_ref.at[h % 2]
        top = None
        for j in range(0, slots, chunk):
            piece = nn(q_ref[h], k_ref[0, h, :, j : j + chunk])
            score[:, j : j + chunk] = piece
            for t in range(0, chunk, 128):
                part = piece[:, t : t + 128]
                top = part if top is None else jnp.maximum(top, part)
        top = jnp.max(top, axis=-1, keepdims=True)
        total = None
        for j in range(0, slots, chunk):
            power = jnp.exp2((score[:, j : j + chunk] - top) * scale).astype(BF16)
            piece = nt(power, v_ref[0, h, :, j : j + chunk])
            total = piece if total is None else total + piece
        weight = total[:, HEAD : HEAD + 1]
        outs.append(total[:, :HEAD] / weight)
        logs.append(top * scale + jnp.log2(weight))
    mixed_ref[0] = jnp.concatenate(outs, axis=1)
    for h, log in enumerate(logs):
        log_ref[0, h] = jnp.broadcast_to(log, log_ref.shape[2:])


def attend(q, k, v, chunk=1024, group=4):
    slots, rows = k.shape[-1], q.shape[1]
    scale = math.log2(math.e) / math.sqrt(HEAD)
    heads = pl.BlockSpec((1, group, PADDED, slots), lambda g: (0, g, 0, 0))
    return pl.pallas_call(
        functools.partial(attend_kernel, chunk, scale),
        grid=(HEADS // group,),
        in_specs=[pl.BlockSpec((group, rows, PADDED), lambda g: (g, 0, 0)), heads, heads],
        out_specs=[
            pl.BlockSpec((1, rows, group * HEAD), lambda g: (0, 0, g)),
            pl.BlockSpec((1, group, rows, 128), lambda g: (0, g, 0, 0)),
        ],
        out_shape=[
            jax.ShapeDtypeStruct((1, rows, HEADS * HEAD), F32),
            jax.ShapeDtypeStruct((1, HEADS, rows, 128), F32),
        ],
        scratch_shapes=[pltpu.VMEM((2, rows, slots), F32)],
        compiler_params=pltpu.CompilerParams(vmem_limit_bytes=VMEM),
        cost_estimate=pl.CostEstimate(
            flops=16 * rows * slots * HEADS * HEAD,
            bytes_accessed=4 * HEADS * PADDED * slots,
            transcendentals=HEADS * rows * slots,
        ),
        name="attend",
    )(q, k, v)


def attend_back_kernel(
    chunk, scale, factor, q_ref, qt_ref, k_ref, v_ref, log_ref, dm_ref, dmt_ref, dq_ref, dk_ref, dv_ref
):
    slots = k_ref.shape[-1]
    grads = []
    for h in range(q_ref.shape[0]):
        log = log_ref[0, h][:, :1]
        mine = slice(h * HEAD, (h + 1) * HEAD)
        total = None
        for j in range(0, slots, chunk):
            keys = k_ref[0, h, :, j : j + chunk]
            probs = jnp.exp2(nn(q_ref[h], keys) * scale - log)
            less = nn(dm_ref[0, h], v_ref[0, h, :, j : j + chunk])
            d_scores = (probs * less).astype(BF16)
            dv_ref[0, mine, j : j + chunk] = nn(dmt_ref[0, mine], probs.astype(BF16)).astype(BF16)
            dk_ref[0, mine, j : j + chunk] = (nn(qt_ref[mine], d_scores) * factor).astype(BF16)
            piece = nt(d_scores, keys[:HEAD])
            total = piece if total is None else total + piece
        grads.append((total * factor).astype(BF16))
    dq_ref[0] = jnp.concatenate(grads, axis=1)


def attend_back(seq, q, qt, k, v, log, dm, dmt, chunk=2048, group=4):
    slots = k.shape[-1]
    rows = q.shape[1]
    scale = math.log2(math.e) / math.sqrt(HEAD)
    heads = pl.BlockSpec((1, group, PADDED, slots), lambda g: (0, g, 0, 0))
    features = pl.BlockSpec((1, group * HEAD, slots), lambda g: (0, g, 0))
    return pl.pallas_call(
        functools.partial(attend_back_kernel, chunk, scale, 1.0 / math.sqrt(HEAD)),
        grid=(HEADS // group,),
        in_specs=[
            pl.BlockSpec((group, rows, PADDED), lambda g: (g, 0, 0)),
            pl.BlockSpec((group * HEAD, rows), lambda g: (g, 0)),
            heads,
            heads,
            pl.BlockSpec((1, group, rows, 128), lambda g: (0, g, 0, 0)),
            pl.BlockSpec((1, group, rows, PADDED), lambda g: (seq, g, 0, 0)),
            pl.BlockSpec((1, group * HEAD, rows), lambda g: (seq, g, 0)),
        ],
        out_specs=[pl.BlockSpec((1, rows, group * HEAD), lambda g: (0, 0, g)), features, features],
        out_shape=[
            jax.ShapeDtypeStruct((1, rows, HEADS * HEAD), BF16),
            jax.ShapeDtypeStruct((1, HEADS * HEAD, slots), BF16),
            jax.ShapeDtypeStruct((1, HEADS * HEAD, slots), BF16),
        ],
        compiler_params=pltpu.CompilerParams(vmem_limit_bytes=VMEM),
        cost_estimate=pl.CostEstimate(
            flops=40 * rows * slots * HEADS * HEAD,
            bytes_accessed=8 * HEADS * PADDED * slots,
            transcendentals=HEADS * rows * slots,
        ),
        name="attend_back",
    )(q, qt, k, v, log, dm, dmt)


def kv_grad_kernel(seqs, *refs):
    grads, normed, (out_ref, total_ref) = refs[: 2 * seqs], refs[2 * seqs : 3 * seqs], refs[3 * seqs :]
    devices = out_ref.shape[0]
    for n in range(2):
        piece = sum(nn(grads[2 * s + n][0], normed[s][0]) for s in range(seqs))

        @pl.when(pl.program_id(0) == 0)
        def _():
            total_ref[n] = piece

        @pl.when(pl.program_id(0) > 0)
        def _():
            total_ref[n] += piece

    @pl.when(pl.program_id(0) == pl.num_programs(0) - 1)
    def _():
        for n in range(2):
            whole = total_ref[n].T
            rows = whole.shape[0] // devices
            for d in range(devices):
                out_ref[d, n * rows : (n + 1) * rows] = whole[d * rows : (d + 1) * rows].astype(BF16)


def kv_grad(grads, normed, devices, tile=1024):
    seqs = len(normed)
    _, slots, width = normed[0].shape
    features = grads[0].shape[1]
    columns = pl.BlockSpec((1, features, tile), lambda j: (0, 0, j))
    shape = (devices, 2 * (width // devices), features)
    return pl.pallas_call(
        functools.partial(kv_grad_kernel, seqs),
        grid=(slots // tile,),
        in_specs=[columns] * (2 * seqs) + [pl.BlockSpec((1, tile, width), lambda j: (0, j, 0))] * seqs,
        out_specs=pl.BlockSpec(shape, lambda j: (0, 0, 0)),
        out_shape=jax.ShapeDtypeStruct(shape, BF16),
        scratch_shapes=[pltpu.VMEM((2, features, width), F32)],
        compiler_params=pltpu.CompilerParams(vmem_limit_bytes=VMEM),
        cost_estimate=pl.CostEstimate(
            flops=8 * seqs * slots * width * features, bytes_accessed=6 * seqs * slots * width, transcendentals=0
        ),
        name="kv_grad",
    )(*grads, *normed)


def query_grad_kernel(seqs, cuts, *refs):
    grads, (base_ref, gain_ref, wq_ref, rest_ref, go_ref, out_ref) = refs[:seqs], refs[seqs:]
    devices = out_ref.shape[0]
    unit, inverse = unit_rows(base_ref[...].astype(F32))
    normed = (unit * gain_ref[...]).astype(BF16)
    query = sum(tn(normed, grad[0]) for grad in grads)
    back = sum(nt(grad[0], wq_ref[...]) for grad in grads)
    latents = norm_back(back, unit, inverse, gain_ref[...]) + rest_ref[...]
    wholes = {"query": query, "out": go_ref[...].astype(F32), "latents": latents}
    for d in range(devices):
        pieces = []
        for what, rows, columns, at, beside in unpack_rest(out_ref.shape[1], cuts):
            whole = wholes[what]
            base = d * (whole.shape[0] // devices)
            out_ref[d, at[0] : at[1], beside[0] : beside[1]] = whole[
                base + rows[0] : base + rows[1], columns[0] : columns[1]
            ].astype(BF16)


def query_grad(grads, base, gain, w_query, rest, grad_out, devices, cuts):
    q_top, q_low, k_rows, l_rows, width, l_width = cuts
    vmem = pl.BlockSpec(memory_space=pltpu.VMEM)
    shape = (devices, q_top + q_low + 2 * k_rows + l_rows, width)
    return pl.pallas_call(
        functools.partial(query_grad_kernel, len(grads), cuts),
        in_specs=[vmem] * (len(grads) + 5),
        out_specs=vmem,
        out_shape=jax.ShapeDtypeStruct(shape, BF16),
        compiler_params=pltpu.CompilerParams(vmem_limit_bytes=VMEM),
        cost_estimate=pl.CostEstimate(
            flops=4 * len(grads) * base.shape[0] * l_width * width, bytes_accessed=12_000_000, transcendentals=0
        ),
        name="query_grad",
    )(*grads, base, gain, w_query, rest, grad_out)


def input_grad_kernel(dk_ref, dv_ref, w_ref, gain_ref, x_ref, *refs):
    out_ref = refs[-1]
    features = dk_ref.shape[1]
    upstream = tn(dk_ref[0], w_ref[:features]) + tn(dv_ref[0], w_ref[features:])
    unit, inverse = unit_rows(x_ref[0].astype(F32))
    out_ref[0] = norm_back(upstream, unit, inverse, gain_ref[...]).astype(BF16)


def input_grad(seq, first, steps, dk, dv, weights, gain, x, into=None, tile=512):
    features = dk.shape[1]
    width = x.shape[-1]
    columns = pl.BlockSpec((1, features, tile), lambda j: (0, 0, first + j))
    rows = pl.BlockSpec((1, tile, width), lambda j: (seq, first + j, 0))
    whole = lambda a: pl.BlockSpec(a.shape, lambda j: (0,) * a.ndim)
    args = [dk, dv, weights, gain, x] + ([] if into is None else [into])
    specs = [columns, columns, whole(weights), whole(gain), rows]
    return pl.pallas_call(
        input_grad_kernel,
        grid=(steps,),
        in_specs=specs + [pl.BlockSpec(memory_space=pl.ANY)] * (len(args) - len(specs)),
        out_specs=rows,
        out_shape=jax.ShapeDtypeStruct(x.shape, BF16),
        input_output_aliases={} if into is None else {5: 0},
        compiler_params=pltpu.CompilerParams(vmem_limit_bytes=VMEM),
        cost_estimate=pl.CostEstimate(
            flops=8 * steps * tile * width * features, bytes_accessed=8 * steps * tile * width, transcendentals=0
        ),
        name="input_grad",
    )(*args)


def gelu_parts(pre):
    cdf = 0.5 * (1.0 + lax.erf(pre * (1.0 / math.sqrt(2.0))))
    slope = cdf + pre * jnp.exp(-0.5 * pre * pre) * (1.0 / math.sqrt(2.0 * math.pi))
    return pre * cdf, slope


def feed_forward_kernel(seqs, *refs):
    mixed = refs[:seqs]
    base_ref, w_out_ref, w_mlp_ref, gain_ref, cot_ref = refs[seqs : seqs + 5]
    latents_ref, g_mlp_ref, g_out_ref, rest_ref, dm_ref, dmt_ref = refs[seqs + 5 : seqs + 11]
    mlp_ref, act_ref, pre_ref, attn_ref, mix_ref = refs[seqs + 11 :]
    _, rows, width = mixed[0].shape
    l_width = base_ref.shape[1]
    w_in_ref, w_back_ref = w_mlp_ref.at[:, :l_width], w_mlp_ref.at[:, l_width:]
    gain = gain_ref[...]
    base = base_ref[...].astype(F32)
    norms, ones, bars = [], [], []
    for s in range(seqs):
        mine = slice(s * rows, (s + 1) * rows)
        mix_ref[mine] = mixed[s][0].astype(BF16)
        x_one = base + nn(mix_ref[mine], w_out_ref[...])
        unit, inverse = unit_rows(x_one)
        mlp_ref[mine] = (unit * gain).astype(BF16)
        norms.append((unit, inverse))
        ones.append(x_one)
    for s in range(seqs):
        mine = slice(s * rows, (s + 1) * rows)
        pre = nn(mlp_ref[mine], w_in_ref[...])
        value, slope = gelu_parts(pre)
        act_ref[mine] = value.astype(BF16)
        pre_ref[mine] = (nt(cot_ref[s], w_back_ref[...]) * slope).astype(BF16)
    for s in range(seqs):
        mine = slice(s * rows, (s + 1) * rows)
        latents_ref[s] = (ones[s] + nn(act_ref[mine], w_back_ref[...])).astype(BF16)
        back = nt(pre_ref[mine], w_in_ref[...])
        bar = cot_ref[s].astype(F32) + norm_back(back, *norms[s], gain)
        attn_ref[mine] = bar.astype(BF16)
        bars.append(bar)
    rest_ref[...] = sum(bars)
    column = lax.broadcasted_iota(jnp.int32, (rows, PADDED - HEAD), 1)
    for s in range(seqs):
        mine = slice(s * rows, (s + 1) * rows)
        d_mixed = nt(attn_ref[mine], w_out_ref[...])
        dmt_ref[s] = d_mixed.T.astype(BF16)
        d_mixed = d_mixed.astype(BF16)
        for h in range(HEADS):
            part = d_mixed[:, h * HEAD : (h + 1) * HEAD]
            centre = -jnp.sum(part.astype(F32) * mixed[s][0, :, h * HEAD : (h + 1) * HEAD], axis=-1, keepdims=True)
            high = centre.astype(BF16).astype(F32)
            middle = (centre - high).astype(BF16).astype(F32)
            low = centre - high - middle
            pieces = jnp.where(column == 0, high, jnp.where(column == 1, middle, jnp.where(column == 2, low, 0.0)))
            dm_ref[s, h] = jnp.concatenate([part, pieces.astype(BF16)], axis=1)
    cot = jnp.concatenate([cot_ref[s] for s in range(seqs)], axis=0)
    devices = g_mlp_ref.shape[0]
    for n, whole in enumerate((tn(mlp_ref[...], pre_ref[...]), tn(act_ref[...], cot))):
        size = l_width // devices
        for d in range(devices):
            g_mlp_ref[d, n * size : (n + 1) * size] = whole[d * size : (d + 1) * size].astype(BF16)
    g_out_ref[...] = tn(mix_ref[...], attn_ref[...]).astype(BF16)


def feed_forward(mixed, base, w_out, w_mlp, gain, cot, devices):
    seqs = len(mixed)
    _, rows, width = mixed[0].shape
    l_width = base.shape[1]
    vmem = pl.BlockSpec(memory_space=pltpu.VMEM)
    shapes = [
        (cot.shape, BF16),
        ((devices, 2 * (l_width // devices), l_width), BF16),
        (w_out.shape, BF16),
        (base.shape, F32),
        ((seqs, HEADS, rows, PADDED), BF16),
        ((seqs, width, rows), BF16),
    ]
    many = seqs * rows
    return pl.pallas_call(
        functools.partial(feed_forward_kernel, seqs),
        in_specs=[vmem] * (seqs + 5),
        out_specs=[vmem] * len(shapes),
        out_shape=[jax.ShapeDtypeStruct(*s) for s in shapes],
        scratch_shapes=[pltpu.VMEM((many, l_width), BF16)] * 4 + [pltpu.VMEM((many, width), BF16)],
        compiler_params=pltpu.CompilerParams(vmem_limit_bytes=VMEM),
        cost_estimate=pl.CostEstimate(
            flops=6 * many * l_width * (width + 2 * l_width), bytes_accessed=24_000_000, transcendentals=0
        ),
        name="feed_forward",
    )(*mixed, base, w_out, w_mlp, gain, cot)


def local(
    byte_inputs,
    lengths,
    key_mask,
    latents_cot,
    latent_array,
    lat_gain,
    query_weight,
    in_gain,
    key_weight,
    value_weight,
    out_weight,
    mlp_gain,
    mlp_in_weight,
    mlp_out_weight,
):
    devices = lax.axis_size("dp")
    grid = Grid(devices)
    seqs, length, width = byte_inputs.shape
    k_rows, q_rows, l_rows = key_weight.shape[0], query_weight.shape[0], latent_array.shape[0]
    l_width = latent_array.shape[1]
    q_top = k_rows if q_rows > k_rows else q_rows // 2
    q_low = q_rows - q_top

    w_mlp = lax.all_gather(jnp.concatenate([mlp_in_weight, mlp_out_weight], axis=1), "dp", axis=0, tiled=True)

    gains = jnp.concatenate([in_gain, lat_gain, mlp_gain])
    sizes = (in_gain.shape[0], lat_gain.shape[0], mlp_gain.shape[0])
    gain_rows = jnp.broadcast_to(jnp.pad(gains, (0, width - gains.shape[0])), (8, width))
    first = Gather(grid, jnp.concatenate([key_weight, value_weight, gain_rows], axis=0), k_rows)
    packed = pack_rest(query_weight, out_weight, latent_array, q_top, jnp.concatenate)
    second = Gather(grid, packed, q_top + k_rows)
    cuts = (q_top, q_low, k_rows, l_rows, width, l_width)
    overlap([first])
    overlap([first, second])
    overlap([first])
    while first.left:
        overlap([first, second])
    positions = jnp.arange(length, dtype=jnp.int32)
    valid = (positions[None, :] < lengths[:, None]) & (key_mask == 1)
    addend = jnp.where(valid, 0.0, MASKED).astype(F32)[:, None]
    places = jnp.stack([grid.found(grid.order_a), grid.found(grid.order_b)])

    def begin(stack):
        ready = prepare_kv(stack, places, sizes)
        return ready, project(0, byte_inputs, ready[1], ready[0], addend)

    (kv_weights, g_in, g_lat, g_mlp), side = overlap([second], begin, first.parts[0])
    sides = [side]
    for s in range(1, seqs):
        sides.append(overlap([second], functools.partial(project, s), byte_inputs, g_in, kv_weights, addend))
    finish([second])
    w_query, w_out, base, q, qt = prepare_q(second.parts[0], g_lat, places, cuts)
    heard = [attend(q, k, v) for _, k, v in sides]
    latents, grad_mlp, grad_out, rest, dm, dmt = feed_forward(
        [mixed for mixed, _ in heard], base, w_out, w_mlp, g_mlp, latents_cot, devices
    )

    mlp_out = Scatter(grid, grad_mlp, q_rows)
    jobs = [mlp_out]
    backs = []
    for s, ((_, k, v), (_, log)) in enumerate(zip(sides, heard)):
        backs.append(overlap(jobs, functools.partial(attend_back, s), q, qt, k, v, log, dm, dmt))
    work = functools.partial(query_grad, devices=devices, cuts=cuts)
    grad_rest = overlap(jobs, work, [back[0] for back in backs], base, g_lat, w_query, rest, grad_out)
    rest_out = Scatter(grid, grad_rest, q_top + k_rows)
    jobs.append(rest_out)
    work = functools.partial(kv_grad, devices=devices)
    grad_kv = overlap(jobs, work, [g for back in backs for g in back[1:]], [side[0] for side in sides])
    kv_out = Scatter(grid, grad_kv, k_rows)
    jobs.append(kv_out)
    inputs_grad = None
    tiles = length // 512
    half = max(tiles // 2, 1)
    for s in range(seqs):
        for at in range(0, tiles, half):
            work = functools.partial(input_grad, s, at, min(half, tiles - at))
            args = (backs[s][1], backs[s][2], kv_weights, g_in, byte_inputs)
            inputs_grad = overlap(jobs, work, *args, *(() if inputs_grad is None else (inputs_grad,)))
    finish(jobs)
    both = jnp.concatenate(mlp_out.parts, axis=0)
    in_grad, back_grad = both[:q_rows], both[q_rows:]
    both = jnp.concatenate(kv_out.parts, axis=0)
    key_grad, value_grad = both[:k_rows], both[k_rows:]
    both = jnp.concatenate(rest_out.parts, axis=0)
    found = {"query": [], "out": [], "latents": []}
    for what, rows_of, columns, at, beside in unpack_rest(both.shape[0], cuts):
        found[what].append((rows_of[0], columns[0], both[at[0] : at[1], beside[0] : beside[1]]))

    def joined(what, axis):
        pieces = sorted(found[what], key=lambda piece: piece[:2])
        return jnp.concatenate([piece[2] for piece in pieces], axis=axis)

    query_grad_mine, out_grad, base_grad = joined("query", 0), joined("out", 1), joined("latents", 1)

    def gain_grad(gain, *pairs):
        total = sum(jnp.sum(g * w.astype(F32), axis=1) for g, w in pairs)
        return total / gain.astype(F32)

    gin_grad = gain_grad(in_gain, (key_grad, key_weight), (value_grad, value_weight))
    glat_grad = gain_grad(lat_gain, (query_grad_mine, query_weight))
    gmlp_grad = gain_grad(mlp_gain, (in_grad, mlp_in_weight))
    return (
        latents,
        inputs_grad,
        base_grad,
        glat_grad,
        query_grad_mine,
        gin_grad,
        key_grad,
        value_grad,
        out_grad,
        gmlp_grad,
        in_grad,
        back_grad,
    )


def solution(mesh):
    in_specs = (
        P("dp", None, None),
        P("dp"),
        P("dp", None),
        P("dp", None, None),
        P("dp", None),
        P("dp"),
        P("dp", None),
        P("dp"),
        P("dp", None),
        P("dp", None),
        P("dp", None),
        P("dp"),
        P("dp", None),
        P("dp", None),
    )
    out_specs = (
        P("dp", None, None),
        P("dp", None, None),
        P("dp", None),
        P("dp"),
        P("dp", None),
        P("dp"),
        P("dp", None),
        P("dp", None),
        P("dp", None),
        P("dp"),
        P("dp", None),
        P("dp", None),
    )
    return jax.shard_map(local, mesh=mesh, in_specs=in_specs, out_specs=out_specs, check_vma=False)
```

```python
import functools
import math

import jax
import jax.numpy as jnp
from jax import lax
from jax.experimental import pallas as pl
from jax.experimental.pallas import tpu as pltpu
from jax.sharding import PartitionSpec as P

HEADS = 8
HEAD = 96
PADDED = 112
MASKED = -1e30
VMEM = 56 * 1024 * 1024
F32 = jnp.float32
BF16 = jnp.bfloat16


def nn(a, b):
    return lax.dot_general(a, b, (((1,), (0,)), ((), ())), preferred_element_type=F32)


def nt(a, b):
    return lax.dot_general(a, b, (((1,), (1,)), ((), ())), preferred_element_type=F32)


def tn(a, b):
    return lax.dot_general(a, b, (((0,), (0,)), ((), ())), preferred_element_type=F32)


def unit_rows(rows):
    centred = rows - jnp.mean(rows, axis=-1, keepdims=True)
    inverse = lax.rsqrt(jnp.mean(centred * centred, axis=-1, keepdims=True) + 1e-05)
    return centred * inverse, inverse


def norm_back(upstream, unit, inverse, gain):
    scaled = upstream * gain
    inner = (
        scaled
        - jnp.mean(scaled, axis=-1, keepdims=True)
        - unit * jnp.mean(scaled * unit, axis=-1, keepdims=True)
    )
    return inverse * inner


def grid_of(devices):
    known = {32: (4, 2, 2), 128: (4, 4, 4)}
    chips = devices // 2
    dims = []
    while chips > 1:
        step = next(f for f in (4, 2, 3, 5, 7, chips) if chips % f == 0)
        dims.append(step)
        chips //= step
    return (*known.get(devices, dims), 2)


class Grid:
    def __init__(self, devices):
        self.devices = devices
        self.dims = grid_of(devices)
        self.strides = tuple(math.prod(self.dims[i + 1 :]) for i in range(len(self.dims)))
        me = lax.axis_index("dp")
        self.mine = tuple((me // s) % k for s, k in zip(self.strides, self.dims))
        self.core = self.mine[-1].astype(jnp.int32).reshape(1)
        near = list(range(1, len(self.dims) - 1))
        self.order_a = (0, *near[::-1])
        self.order_b = (0, *near)

    def shift(self, dim, r):
        k, s = self.dims[dim], self.strides[dim]
        pairs = []
        for i in range(self.devices):
            at = (i // s) % k
            pairs.append((i, i + (((at + r) % k) - at) * s))
        return pairs

    def send(self, array, dim, r):
        return lax.ppermute(array, "dp", self.shift(dim, r))

    def swap(self, array, dim):
        k, s = self.dims[dim], self.strides[dim]
        firsts = [i for i in range(self.devices) if (i // s) % k == 0]
        groups = [[i + n * s for n in range(k)] for i in firsts]
        return lax.all_to_all(array, "dp", 0, 0, axis_index_groups=groups)

    def found(self, order):
        dims = self.dims[:-1]
        sizes = [dims[dim] for dim in order]
        index = jnp.zeros((1,) * len(dims), jnp.int32)
        for n, dim in enumerate(order):
            step = math.prod(sizes[:n])
            away = (jnp.arange(dims[dim], dtype=jnp.int32) - self.mine[dim]) % dims[dim]
            shape = [1] * len(dims)
            shape[dim] = dims[dim]
            index = index + (away * step).reshape(shape)
        return index.reshape(-1)


class Gather:
    def __init__(self, grid, block, cut):
        self.grid, self.cut, self.parts = grid, cut, [block[None]]
        last = len(grid.dims) - 1
        self.left = [*zip(grid.order_a, grid.order_b), (last, last)]

    def sends(self):
        one, other = self.dims = self.left.pop(0)
        if one == other:
            self.parts = [jnp.concatenate(self.parts, axis=1)] if len(self.parts) == 2 else self.parts
        elif len(self.parts) == 1:
            self.parts = jnp.split(self.parts[0], [self.cut], axis=1)
        return self.parts

    def exchange(self, sent):
        sizes = self.grid.dims
        return [
            [part] + [self.grid.send(part, dim, -r) for r in range(1, sizes[dim])]
            for dim, part in zip(self.dims, sent)
        ]

    def receive(self, got):
        self.parts = [jnp.concatenate(part, axis=0) for part in got] if self.left else got[0]


class Cores:
    def __init__(self, grid, kept, sent):
        self.grid, self.value, self.left = grid, [kept, sent], [True]

    def sends(self):
        self.left.pop()
        return self.value

    def exchange(self, sent):
        return [sent[0], self.grid.send(sent[1], len(self.grid.dims) - 1, 1)]

    def receive(self, got):
        self.value = (got[0].astype(F32) + got[1].astype(F32)).astype(got[0].dtype)


class Scatter:
    def __init__(self, grid, parts):
        self.grid = grid
        self.parts = [part.reshape(*grid.dims[:-1], *part.shape[1:]) for part in parts]
        self.left = [*zip(grid.order_a, grid.order_b)][::-1]
        self.rest = [list(range(len(grid.dims) - 1)) for _ in parts]

    def sends(self):
        self.dims = self.left.pop(0)
        if not self.left and len(self.parts) == 2:
            self.parts = [jnp.concatenate(self.parts, axis=1)]
        if not self.left:
            return self.parts
        sent = []
        for part, dim, rest in zip(self.parts, self.dims, self.rest):
            axis, k, me = rest.index(dim), self.grid.dims[dim], self.grid.mine[dim]
            rest.remove(dim)
            sent.append(
                [lax.dynamic_index_in_dim(part, (me + r) % k, axis, keepdims=False) for r in range(k)]
            )
        return sent

    def exchange(self, sent):
        if not self.left:
            return [self.grid.swap(part, self.dims[0]) for part in sent]
        return [
            part[:1] + [self.grid.send(piece, dim, r) for r, piece in enumerate(part) if r]
            for dim, part in zip(self.dims, sent)
        ]

    def receive(self, got):
        if not self.left:
            self.parts = [jnp.sum(part.astype(F32), axis=0) for part in got]
            return
        totals = [sum(piece.astype(F32) for piece in part) for part in got]
        self.parts = [total.astype(got[0][0].dtype) for total in totals]


def window(starts, ends, work=None, *args):
    sent, args = lax.optimization_barrier(([job.sends() for job in starts], args))
    for job, parts in zip(starts, sent):
        job.running = job.exchange(parts)
    out = work(*args) if work else ()
    got, out = lax.optimization_barrier(([job.running for job in ends], out))
    for job, parts in zip(ends, got):
        job.receive(parts)
    return out


def by_core(core_ref, one, other):
    first = core_ref[0] == 0
    return jnp.where(first, one, other), jnp.where(first, other, one)


def prepare_kv_kernel(cuts, core_ref, place_ref, own_ref, other_ref, wt_ref, gin_ref, glat_ref, gmlp_ref, kv_ref):
    chips, _, width = own_ref.shape
    k_rows = width // (2 * chips)
    lines = []
    for chip in range(chips):
        at = [place_ref[n, chip] for n in range(2)]
        keys = by_core(core_ref, own_ref[at[0], :k_rows], other_ref[at[0], :k_rows])
        values = by_core(core_ref, own_ref[at[1], k_rows : 2 * k_rows], other_ref[at[1], k_rows : 2 * k_rows])
        both = by_core(core_ref, own_ref[at[1], 2 * k_rows :], other_ref[at[1], 2 * k_rows :])
        for n in range(2):
            mine = slice((2 * chip + n) * k_rows, (2 * chip + n + 1) * k_rows)
            kv_ref[mine, :width] = keys[n]
            kv_ref[mine, width:] = values[n]
            lines.append(both[n][:1].astype(F32))
    first = 0
    for ref, size in zip((gin_ref, glat_ref, gmlp_ref), cuts):
        ref[...] = jnp.concatenate([line[:, first : first + size] for line in lines], axis=1)
        first += size
    for c in range(0, wt_ref.shape[0], width):
        wt_ref[c : c + width] = kv_ref[:, c : c + width].T


def prepare_kv(core, places, stacks, cuts):
    width = stacks[0].shape[-1]
    devices = 2 * stacks[0].shape[0]
    vmem = pl.BlockSpec(memory_space=pltpu.VMEM)
    smem = pl.BlockSpec(memory_space=pltpu.SMEM)
    shapes = [((2 * width, width), BF16)] + [((1, devices * size), F32) for size in cuts]
    return pl.pallas_call(
        functools.partial(prepare_kv_kernel, cuts),
        in_specs=[smem, smem, vmem, vmem],
        out_specs=[vmem] * len(shapes),
        out_shape=[jax.ShapeDtypeStruct(*s) for s in shapes],
        scratch_shapes=[pltpu.VMEM((width, 2 * width), BF16)],
        compiler_params=pltpu.CompilerParams(vmem_limit_bytes=VMEM),
        cost_estimate=pl.CostEstimate(flops=0, bytes_accessed=12_000_000, transcendentals=0),
        name="prepare_kv",
    )(core, places, *stacks)


def unpack_rest(cuts):
    q_top, q_low, k_rows, l_rows, width, l_width = cuts
    spare = 2 * width - l_width
    second = q_top + k_rows
    third = second + k_rows
    found = [
        ("query", (0, q_top), (0, width), (0, q_top), (0, width)),
        ("out", (0, k_rows), (0, width), (q_top, second), (0, width)),
        ("out", (0, k_rows), (width, l_width), (second, third), (0, l_width - width)),
        ("query", (q_top, q_top + q_low), (0, width), (third, third + q_low), (0, width)),
        ("latents", (0, l_rows), (0, width), (third + q_low, third + q_low + l_rows), (0, width)),
    ]
    for n, at in enumerate(range(width, l_width, spare)):
        end = min(at + spare, l_width)
        start = second + n * l_rows
        found.append(
            ("latents", (0, l_rows), (at, end), (start, start + l_rows), (l_width - width, l_width - width + end - at))
        )
    return found


def prepare_q_kernel(cuts, core_ref, place_ref, own_ref, other_ref, glat_ref, wq_ref, lat_ref, q_ref, qt_ref):
    chips, _, width = own_ref.shape
    q_top, q_low, _, l_rows, _, l_width = cuts
    q_rows = q_top + q_low
    head = q_rows + l_rows
    pieces = [
        (0, wq_ref, q_rows, (0, q_top), (0, width), 0),
        (1, wq_ref, q_rows, (q_top, q_rows), (0, width), q_top),
        (1, lat_ref, l_rows, (q_rows, head), (0, width), 0),
        (1, lat_ref, l_rows, (head, head + l_rows), (width, l_width), 0),
    ]
    for chip in range(chips):
        for part, ref, size, (first, last), (left, right), row in pieces:
            place = place_ref[part, chip]
            span = slice(0, right - left)
            both = by_core(core_ref, own_ref[place, first:last, span], other_ref[place, first:last, span])
            for n in range(2):
                base = (2 * chip + n) * size + row
                ref[base : base + last - first, left:right] = both[n]
    unit, _ = unit_rows(lat_ref[...].astype(F32))
    query = nn((unit * glat_ref[...]).astype(BF16), wq_ref[...])
    qt_ref[...] = query.T.astype(BF16)
    query = query.astype(BF16)
    column = lax.broadcasted_iota(jnp.int32, (query.shape[0], PADDED - HEAD), 1)
    ones = jnp.where(column == 0, 1.0, 0.0).astype(BF16)
    for h in range(HEADS):
        q_ref[h] = jnp.concatenate([query[:, h * HEAD : (h + 1) * HEAD], ones], axis=1)


def prepare_q(core, places, stacks, gain, cuts):
    devices = 2 * stacks[0].shape[0]
    q_top, q_low, _, l_rows, width, l_width = cuts
    rows = devices * l_rows
    vmem = pl.BlockSpec(memory_space=pltpu.VMEM)
    smem = pl.BlockSpec(memory_space=pltpu.SMEM)
    shapes = [(devices * (q_top + q_low), width), (rows, l_width), (HEADS, rows, PADDED), (width, rows)]
    return pl.pallas_call(
        functools.partial(prepare_q_kernel, cuts),
        in_specs=[smem, smem, vmem, vmem, vmem],
        out_specs=[vmem] * len(shapes),
        out_shape=[jax.ShapeDtypeStruct(s, BF16) for s in shapes],
        compiler_params=pltpu.CompilerParams(vmem_limit_bytes=VMEM),
        cost_estimate=pl.CostEstimate(flops=0, bytes_accessed=12_000_000, transcendentals=0),
        name="prepare_q",
    )(core, places, *stacks, gain)


def project_kernel(x_ref, gain_ref, w_ref, addend_ref, *refs):
    normed_ref, k_ref, v_ref = refs[-3:]
    unit, _ = unit_rows(x_ref[0].astype(F32))
    normed = (unit * gain_ref[...]).astype(BF16)
    normed_ref[0] = normed
    slots = normed.shape[0]
    both = nt(w_ref[...], normed).astype(BF16)
    row = lax.broadcasted_iota(jnp.int32, (PADDED - HEAD, slots), 0)
    mask_rows = jnp.where(row == 0, jnp.broadcast_to(addend_ref[0], row.shape), 0.0).astype(BF16)
    one_rows = jnp.where(row < 3, 1.0, 0.0).astype(BF16)
    for h in range(HEADS):
        k_ref[0, h, :HEAD] = both[h * HEAD : (h + 1) * HEAD]
        k_ref[0, h, HEAD:] = mask_rows
        v_ref[0, h, :HEAD] = both[(HEADS + h) * HEAD : (HEADS + h + 1) * HEAD]
        v_ref[0, h, HEAD:] = one_rows


def project(first, steps, tile, x, gain, weights, addend, *into):
    seqs, slots, width = x.shape
    tiles = slots // tile
    at = lambda i: ((first + i) // tiles, (first + i) % tiles)
    rows = pl.BlockSpec((1, tile, width), lambda i: (*at(i), 0))
    heads = pl.BlockSpec((1, HEADS, PADDED, tile), lambda i: (at(i)[0], 0, 0, at(i)[1]))
    whole = lambda a: pl.BlockSpec(a.shape, lambda i: (0,) * a.ndim)
    mask = pl.BlockSpec((1, 1, tile), lambda i: (at(i)[0], 0, at(i)[1]))
    return pl.pallas_call(
        project_kernel,
        grid=(steps,),
        in_specs=[rows, whole(gain), whole(weights), mask] + [pl.BlockSpec(memory_space=pl.ANY)] * len(into),
        out_specs=[rows, heads, heads],
        out_shape=[
            jax.ShapeDtypeStruct((seqs, slots, width), BF16),
            jax.ShapeDtypeStruct((seqs, HEADS, PADDED, slots), BF16),
            jax.ShapeDtypeStruct((seqs, HEADS, PADDED, slots), BF16),
        ],
        input_output_aliases={4 + n: n for n in range(len(into))},
        compiler_params=pltpu.CompilerParams(vmem_limit_bytes=VMEM),
        cost_estimate=pl.CostEstimate(
            flops=8 * steps * tile * width * width, bytes_accessed=10 * steps * tile * width, transcendentals=0
        ),
        name="project",
    )(x, gain, weights, addend, *into)


def attend_kernel(chunk, scale, q_ref, k_ref, v_ref, mixed_ref, power_ref, weight_ref, score_ref):
    slots = k_ref.shape[-1]
    outs = []
    lane = lax.broadcasted_iota(jnp.int32, weight_ref.shape[2:], 1)
    weights = jnp.zeros(lane.shape, F32)
    for h in range(q_ref.shape[0]):
        score = score_ref.at[h % 2]
        top = None
        for j in range(0, slots, chunk):
            piece = nn(q_ref[h], k_ref[0, h, :, j : j + chunk])
            score[:, j : j + chunk] = piece
            for t in range(0, chunk, 128):
                part = piece[:, t : t + 128]
                top = part if top is None else jnp.maximum(top, part)
        top = jnp.max(top, axis=-1, keepdims=True)
        total = None
        for j in range(0, slots, chunk):
            power = jnp.exp2((score[:, j : j + chunk] - top) * scale).astype(BF16)
            power_ref[0, h, :, j : j + chunk] = power
            piece = nt(power, v_ref[0, h, :, j : j + chunk])
            total = piece if total is None else total + piece
        weight = 1.0 / total[:, HEAD : HEAD + 1]
        outs.append(total[:, :HEAD] * weight)
        weights = jnp.where(lane == h, weight, weights)
    mixed_ref[0] = jnp.concatenate(outs, axis=1)
    weight_ref[0, 0] = weights


def attend(q, k, v, chunk=1024, group=4):
    seqs, slots, rows = k.shape[0], k.shape[-1], q.shape[1]
    scale = math.log2(math.e) / math.sqrt(HEAD)
    heads = pl.BlockSpec((1, group, PADDED, slots), lambda s, g: (s, g, 0, 0))
    return pl.pallas_call(
        functools.partial(attend_kernel, chunk, scale),
        grid=(seqs, HEADS // group),
        in_specs=[pl.BlockSpec((group, rows, PADDED), lambda s, g: (g, 0, 0)), heads, heads],
        out_specs=[
            pl.BlockSpec((1, rows, group * HEAD), lambda s, g: (s, 0, g)),
            pl.BlockSpec((1, group, rows, slots), lambda s, g: (s, g, 0, 0)),
            pl.BlockSpec((1, 1, rows, 128), lambda s, g: (s, g, 0, 0)),
        ],
        out_shape=[
            jax.ShapeDtypeStruct((seqs, rows, HEADS * HEAD), F32),
            jax.ShapeDtypeStruct((seqs, HEADS, rows, slots), BF16),
            jax.ShapeDtypeStruct((seqs, HEADS // group, rows, 128), F32),
        ],
        scratch_shapes=[pltpu.VMEM((2, rows, slots), F32)],
        compiler_params=pltpu.CompilerParams(vmem_limit_bytes=VMEM),
        cost_estimate=pl.CostEstimate(
            flops=16 * seqs * rows * slots * HEADS * HEAD,
            bytes_accessed=4 * seqs * HEADS * PADDED * slots,
            transcendentals=seqs * HEADS * rows * slots,
        ),
        name="attend",
    )(q, k, v)


def attend_back_kernel(factor, qt_ref, k_ref, v_ref, power_ref, dm_ref, dmt_ref, dq_ref, dk_ref, dv_ref):
    grads = []
    for h in range(power_ref.shape[1]):
        mine = slice(h * HEAD, (h + 1) * HEAD)
        power = power_ref[0, h]
        d_scores = (power.astype(F32) * nn(dm_ref[0, h], v_ref[0, h])).astype(BF16)
        dv_ref[0, mine] = nn(dmt_ref[0, mine], power).astype(BF16)
        dk_ref[0, mine] = (nn(qt_ref[mine], d_scores) * factor).astype(BF16)
        grads.append((nt(d_scores, k_ref[0, h, :HEAD]) * factor).astype(BF16))
    dq_ref[0] = jnp.concatenate(grads, axis=1)


def attend_back(seq, qt, k, v, power, dm, dmt, group=4):
    slots, rows = k.shape[-1], qt.shape[1]
    heads = pl.BlockSpec((1, group, PADDED, slots), lambda g: (seq, g, 0, 0))
    features = pl.BlockSpec((1, group * HEAD, slots), lambda g: (0, g, 0))
    return pl.pallas_call(
        functools.partial(attend_back_kernel, 1.0 / math.sqrt(HEAD)),
        grid=(HEADS // group,),
        in_specs=[
            pl.BlockSpec((group * HEAD, rows), lambda g: (g, 0)),
            heads,
            heads,
            pl.BlockSpec((1, group, rows, slots), lambda g: (seq, g, 0, 0)),
            pl.BlockSpec((1, group, rows, PADDED), lambda g: (seq, g, 0, 0)),
            pl.BlockSpec((1, group * HEAD, rows), lambda g: (seq, g, 0)),
        ],
        out_specs=[pl.BlockSpec((1, rows, group * HEAD), lambda g: (0, 0, g)), features, features],
        out_shape=[
            jax.ShapeDtypeStruct((1, rows, HEADS * HEAD), BF16),
            jax.ShapeDtypeStruct((1, HEADS * HEAD, slots), BF16),
            jax.ShapeDtypeStruct((1, HEADS * HEAD, slots), BF16),
        ],
        compiler_params=pltpu.CompilerParams(vmem_limit_bytes=VMEM),
        cost_estimate=pl.CostEstimate(
            flops=32 * rows * slots * HEADS * HEAD,
            bytes_accessed=8 * HEADS * PADDED * slots + 2 * HEADS * rows * slots,
            transcendentals=0,
        ),
        name="attend_back",
    )(qt, k, v, power, dm, dmt)


def weight_grad_kernel(seqs, core_ref, *refs):
    grads, normed_ref, (kept_ref, sent_ref, total_ref) = refs[:seqs], refs[seqs], refs[seqs + 1 :]
    chips, rows, _ = kept_ref.shape
    piece = sum(nn(grad[0], normed_ref[s]) for s, grad in enumerate(grads))

    @pl.when(pl.program_id(0) == 0)
    def _():
        total_ref[...] = piece

    @pl.when(pl.program_id(0) > 0)
    def _():
        total_ref[...] += piece

    @pl.when(pl.program_id(0) == pl.num_programs(0) - 1)
    def _():
        whole = total_ref[...].T
        for chip in range(chips):
            at = 2 * chip * rows
            kept, sent = by_core(core_ref, whole[at : at + rows], whole[at + rows : at + 2 * rows])
            kept_ref[chip] = kept.astype(BF16)
            sent_ref[chip] = sent.astype(BF16)


def weight_grad(core, grads, normed, devices, tile=1024):
    seqs, slots, width = normed.shape
    features = grads[0].shape[1]
    columns = pl.BlockSpec((1, features, tile), lambda j: (0, 0, j))
    shape = (devices // 2, width // devices, features)
    return pl.pallas_call(
        functools.partial(weight_grad_kernel, seqs),
        grid=(slots // tile,),
        in_specs=[pl.BlockSpec(memory_space=pltpu.SMEM)]
        + [columns] * seqs
        + [pl.BlockSpec((seqs, tile, width), lambda j: (0, j, 0))],
        out_specs=[pl.BlockSpec(shape, lambda j: (0, 0, 0))] * 2,
        out_shape=[jax.ShapeDtypeStruct(shape, BF16)] * 2,
        scratch_shapes=[pltpu.VMEM((features, width), F32)],
        compiler_params=pltpu.CompilerParams(vmem_limit_bytes=VMEM),
        cost_estimate=pl.CostEstimate(
            flops=4 * seqs * slots * width * features, bytes_accessed=4 * seqs * slots * width, transcendentals=0
        ),
        name="weight_grad",
    )(core, *grads, normed)


def query_grad_kernel(seqs, cuts, core_ref, *refs):
    grads, (base_ref, gain_ref, wq_ref, rest_ref, go_ref, kept_ref, sent_ref) = refs[:seqs], refs[seqs:]
    chips = kept_ref.shape[0]
    unit, inverse = unit_rows(base_ref[...].astype(F32))
    normed = (unit * gain_ref[...]).astype(BF16)
    query = sum(tn(normed, grad[0]) for grad in grads)
    back = sum(nt(grad[0], wq_ref[...]) for grad in grads)
    latents = norm_back(back, unit, inverse, gain_ref[...]) + rest_ref[...]
    wholes = {"query": query, "out": go_ref[...].astype(F32), "latents": latents}
    for chip in range(chips):
        for what, rows, columns, at, beside in unpack_rest(cuts):
            whole = wholes[what]
            size = whole.shape[0] // (2 * chips)
            pieces = [
                whole[base + rows[0] : base + rows[1], columns[0] : columns[1]]
                for base in (2 * chip * size, (2 * chip + 1) * size)
            ]
            for ref, piece in zip((kept_ref, sent_ref), by_core(core_ref, *pieces)):
                ref[chip, at[0] : at[1], beside[0] : beside[1]] = piece.astype(BF16)


def query_grad(core, grads, base, gain, w_query, rest, grad_out, devices, cuts):
    q_top, q_low, k_rows, l_rows, width, l_width = cuts
    vmem = pl.BlockSpec(memory_space=pltpu.VMEM)
    shape = (devices // 2, q_top + q_low + 2 * k_rows + l_rows, width)
    return pl.pallas_call(
        functools.partial(query_grad_kernel, len(grads), cuts),
        in_specs=[pl.BlockSpec(memory_space=pltpu.SMEM)] + [vmem] * (len(grads) + 5),
        out_specs=[vmem] * 2,
        out_shape=[jax.ShapeDtypeStruct(shape, BF16)] * 2,
        compiler_params=pltpu.CompilerParams(vmem_limit_bytes=VMEM),
        cost_estimate=pl.CostEstimate(
            flops=4 * len(grads) * base.shape[0] * l_width * width, bytes_accessed=12_000_000, transcendentals=0
        ),
        name="query_grad",
    )(core, *grads, base, gain, w_query, rest, grad_out)


def input_grad_kernel(dk_ref, dv_ref, w_ref, gain_ref, x_ref, *refs):
    out_ref = refs[-1]
    features = dk_ref.shape[1]
    upstream = tn(dk_ref[0], w_ref[:features]) + tn(dv_ref[0], w_ref[features:])
    unit, inverse = unit_rows(x_ref[0].astype(F32))
    out_ref[0] = norm_back(upstream, unit, inverse, gain_ref[...]).astype(BF16)


def input_grad(seq, first, steps, dk, dv, weights, gain, x, into=None, tile=512):
    features = dk.shape[1]
    width = x.shape[-1]
    columns = pl.BlockSpec((1, features, tile), lambda j: (0, 0, first + j))
    rows = pl.BlockSpec((1, tile, width), lambda j: (seq, first + j, 0))
    whole = lambda a: pl.BlockSpec(a.shape, lambda j: (0,) * a.ndim)
    args = [dk, dv, weights, gain, x] + ([] if into is None else [into])
    specs = [columns, columns, whole(weights), whole(gain), rows]
    return pl.pallas_call(
        input_grad_kernel,
        grid=(steps,),
        in_specs=specs + [pl.BlockSpec(memory_space=pl.ANY)] * (len(args) - len(specs)),
        out_specs=rows,
        out_shape=jax.ShapeDtypeStruct(x.shape, BF16),
        input_output_aliases={} if into is None else {5: 0},
        compiler_params=pltpu.CompilerParams(vmem_limit_bytes=VMEM),
        cost_estimate=pl.CostEstimate(
            flops=8 * steps * tile * width * features, bytes_accessed=8 * steps * tile * width, transcendentals=0
        ),
        name="input_grad",
    )(*args)


def gelu_parts(pre):
    cdf = 0.5 * (1.0 + lax.erf(pre * (1.0 / math.sqrt(2.0))))
    slope = cdf + pre * jnp.exp(-0.5 * pre * pre) * (1.0 / math.sqrt(2.0 * math.pi))
    return pre * cdf, slope


def feed_forward_kernel(
    core_ref, mixed_ref, weight_ref, base_ref, late_ref, gain_ref, cot_ref,
    latents_out, kept_out, sent_out, g_out_out, rest_out, dm_ref, dmt_ref,
    w_in_ref, w_back_ref, side_ref, w_out_ref, mlp_ref, act_ref, pre_ref, attn_ref, mix_ref,
    latents_ref, kept_ref, sent_ref, g_out_ref, rest_ref, come, go,
):
    seqs, rows, width = mixed_ref.shape
    l_width = base_ref.shape[1]
    arrivals = [
        pltpu.make_async_copy(late_ref.at[:, first : first + ref.shape[1]], ref, come.at[n])
        for n, (ref, first) in enumerate(((side_ref, 2 * l_width), (w_in_ref, 0), (w_back_ref, l_width)))
    ]
    for copy in arrivals:
        copy.start()
    pairs = [
        (latents_ref, latents_out), (rest_ref, rest_out), (kept_ref, kept_out), (sent_ref, sent_out), (g_out_ref, g_out_out)
    ]
    leaves = [pltpu.make_async_copy(ref, out, go.at[n]) for n, (ref, out) in enumerate(pairs)]

    gain = gain_ref[...]
    base = base_ref[...].astype(F32)
    for s in range(seqs):
        mix_ref[s * rows : (s + 1) * rows] = mixed_ref[s].astype(BF16)
    arrivals[0].wait()
    chips = kept_ref.shape[0]
    devices = 2 * chips
    u = width // devices // 3
    part = side_ref.shape[1]
    for d in range(devices):
        for n in range(3 * l_width // part):
            block = side_ref[(d * (side_ref.shape[0] // devices)) + n * u : d * (side_ref.shape[0] // devices) + (n + 1) * u]
            at = n * part
            while at < (n + 1) * part:
                row, left = divmod(at, l_width)
                size = min(l_width - left, (n + 1) * part - at)
                base_row = 3 * u * d + row * u
                w_out_ref[base_row : base_row + u, left : left + size] = block[:, at - n * part : at - n * part + size]
                at += size
    norms, ones, bars = [], [], []
    for s in range(seqs):
        mine = slice(s * rows, (s + 1) * rows)
        x_one = base + nn(mix_ref[mine], w_out_ref[...])
        unit, inverse = unit_rows(x_one)
        mlp_ref[mine] = (unit * gain).astype(BF16)
        norms.append((unit, inverse))
        ones.append(x_one)
    arrivals[1].wait()
    arrivals[2].wait()
    for s in range(seqs):
        mine = slice(s * rows, (s + 1) * rows)
        pre = nn(mlp_ref[mine], w_in_ref[...])
        value, slope = gelu_parts(pre)
        act_ref[mine] = value.astype(BF16)
        pre_ref[mine] = (nt(cot_ref[s], w_back_ref[...]) * slope).astype(BF16)
    for s in range(seqs):
        mine = slice(s * rows, (s + 1) * rows)
        latents_ref[s] = (ones[s] + nn(act_ref[mine], w_back_ref[...])).astype(BF16)
        back = nt(pre_ref[mine], w_in_ref[...])
        bar = cot_ref[s].astype(F32) + norm_back(back, *norms[s], gain)
        attn_ref[mine] = bar.astype(BF16)
        bars.append(bar)
    rest_ref[...] = sum(bars)
    leaves[0].start()
    leaves[1].start()
    cot = jnp.concatenate([cot_ref[s] for s in range(seqs)], axis=0)
    size = l_width // devices
    for n, whole in enumerate((tn(mlp_ref[...], pre_ref[...]), tn(act_ref[...], cot))):
        for chip in range(chips):
            at = 2 * chip * size
            both = by_core(core_ref, whole[at : at + size], whole[at + size : at + 2 * size])
            for ref, block in zip((kept_ref, sent_ref), both):
                ref[chip, n * size : (n + 1) * size] = block.astype(BF16)
    leaves[2].start()
    leaves[3].start()
    g_out_ref[...] = tn(mix_ref[...], attn_ref[...]).astype(BF16)
    leaves[4].start()
    column = lax.broadcasted_iota(jnp.int32, (rows, PADDED - HEAD), 1)
    group = HEADS // weight_ref.shape[1]
    for s in range(seqs):
        mine = slice(s * rows, (s + 1) * rows)
        d_mixed = nt(attn_ref[mine], w_out_ref[...])
        parts = []
        for h in range(HEADS):
            weight = weight_ref[s, h // group, :, h % group : h % group + 1]
            parts.append(d_mixed[:, h * HEAD : (h + 1) * HEAD] * weight)
        dmt_ref[s] = jnp.concatenate(parts, axis=1).T.astype(BF16)
        for h, part in enumerate(parts):
            part = part.astype(BF16)
            centre = -jnp.sum(part.astype(F32) * mixed_ref[s, :, h * HEAD : (h + 1) * HEAD], axis=-1, keepdims=True)
            high = centre.astype(BF16).astype(F32)
            middle = (centre - high).astype(BF16).astype(F32)
            low = centre - high - middle
            pieces = jnp.where(column == 0, high, jnp.where(column == 1, middle, jnp.where(column == 2, low, 0.0)))
            dm_ref[s, h] = jnp.concatenate([part, pieces.astype(BF16)], axis=1)
    for copy in leaves:
        copy.wait()


def feed_forward(core, mixed, weight, base, late, gain, cot, devices):
    seqs, rows, width = mixed.shape
    l_width = base.shape[1]
    vmem = pl.BlockSpec(memory_space=pltpu.VMEM)
    anywhere = pl.BlockSpec(memory_space=pl.ANY)
    blocks = ((devices // 2, 2 * (l_width // devices), l_width), BF16)
    moved = [(cot.shape, BF16), blocks, blocks, ((width, l_width), BF16), (base.shape, F32)]
    shapes = moved + [((seqs, HEADS, rows, PADDED), BF16), ((seqs, width, rows), BF16)]
    many = seqs * rows
    square = pltpu.VMEM((l_width, l_width), BF16)
    return pl.pallas_call(
        feed_forward_kernel,
        in_specs=[pl.BlockSpec(memory_space=pltpu.SMEM), vmem, vmem, vmem, anywhere, vmem, vmem],
        out_specs=[anywhere] * len(moved) + [vmem] * 2,
        out_shape=[jax.ShapeDtypeStruct(*s) for s in shapes],
        scratch_shapes=[
            square,
            square,
            pltpu.VMEM((l_width, late.shape[1] - 2 * l_width), BF16),
            pltpu.VMEM((width, l_width), BF16),
            *[pltpu.VMEM((many, l_width), BF16)] * 4,
            pltpu.VMEM((many, width), BF16),
            *[pltpu.VMEM(*s) for s in moved],
            pltpu.SemaphoreType.DMA((3,)),
            pltpu.SemaphoreType.DMA((len(moved),)),
        ],
        compiler_params=pltpu.CompilerParams(vmem_limit_bytes=VMEM),
        cost_estimate=pl.CostEstimate(
            flops=6 * many * l_width * (width + 2 * l_width), bytes_accessed=24_000_000, transcendentals=0
        ),
        name="feed_forward",
    )(core, mixed, weight, base, late, gain, cot)


def local(
    byte_inputs,
    lengths,
    key_mask,
    latents_cot,
    latent_array,
    lat_gain,
    query_weight,
    in_gain,
    key_weight,
    value_weight,
    out_weight,
    mlp_gain,
    mlp_in_weight,
    mlp_out_weight,
):
    devices = lax.axis_size("dp")
    grid = Grid(devices)
    seqs, length, width = byte_inputs.shape
    k_rows, q_rows, l_rows = key_weight.shape[0], query_weight.shape[0], latent_array.shape[0]
    l_width = latent_array.shape[1]
    q_top = k_rows if q_rows > k_rows else q_rows // 2
    q_low = q_rows - q_top

    unit_size = k_rows // 3
    side = jnp.concatenate([out_weight[n * unit_size : (n + 1) * unit_size] for n in range(3)], axis=1)
    count = q_rows // unit_size
    late_width = side.shape[1] // count
    side = jnp.concatenate([side[:, n * late_width : (n + 1) * late_width] for n in range(count)], axis=0)
    late = lax.all_gather(
        jnp.concatenate([mlp_in_weight, mlp_out_weight, side], axis=1), "dp", axis=0, tiled=True
    )

    gains = jnp.concatenate([in_gain, lat_gain, mlp_gain])
    sizes = (in_gain.shape[0], lat_gain.shape[0], mlp_gain.shape[0])
    gain_rows = jnp.broadcast_to(jnp.pad(gains, (0, width - gains.shape[0])), (8, width))
    first = Gather(grid, jnp.concatenate([key_weight, value_weight, gain_rows], axis=0), k_rows)
    tail = jnp.pad(latent_array[:, width:], ((0, 0), (0, 2 * width - l_width)))
    packed = jnp.concatenate([query_weight, latent_array[:, :width], tail], axis=0)
    second = Gather(grid, packed, q_top)
    cuts = (q_top, q_low, k_rows, l_rows, width, l_width)
    window([first], [first])
    while len(first.left) > 2:
        window([first], [first])
    window([first, second], [first, second])
    window([first, second], [first])
    positions = jnp.arange(length, dtype=jnp.int32)
    valid = (positions[None, :] < lengths[:, None]) & (key_mask == 1)
    addend = jnp.where(valid, 0.0, MASKED).astype(F32)[:, None]
    places = jnp.stack([grid.found(grid.order_a), grid.found(grid.order_b)])
    core = grid.core
    kv_weights, g_in, g_lat, g_mlp = window(
        [], [second], functools.partial(prepare_kv, cuts=sizes), core, places, first.parts
    )
    tile = 512
    tiles = seqs * (length // tile)
    lag = max(tiles // 4, 1)
    given = (byte_inputs, g_in, kv_weights, addend)
    while len(second.left) > 1:
        made = window([second], [second], functools.partial(project, 0, tiles - lag, tile), *given)
    normed, k, v = window(
        [second], [second], functools.partial(project, tiles - lag, lag, tile), *given, *made
    )
    w_query, base, q, qt = prepare_q(core, places, second.parts, g_lat, cuts)
    mixed, power, weight = attend(q, k, v)
    latents, kept, sent, grad_out, rest, dm, dmt = feed_forward(
        core, mixed, weight, base, late, g_mlp, latents_cot, devices
    )

    mlp_cores = Cores(grid, kept, sent)
    given = (qt, k, v, power, dm, dmt)
    backs = [window([mlp_cores], [mlp_cores], functools.partial(attend_back, 0), *given)]
    mlp_out = Scatter(grid, jnp.split(mlp_cores.value, [q_rows], axis=1))
    for s in range(1, seqs):
        backs.append(window([mlp_out] if s == 1 else [], [], functools.partial(attend_back, s), *given))
    d_query, d_keys, d_values = zip(*backs)
    work = functools.partial(query_grad, devices=devices, cuts=cuts)
    rest_cores = Cores(
        grid, *window([], [mlp_out], work, core, d_query, base, g_lat, w_query, rest, grad_out)
    )
    work = functools.partial(weight_grad, devices=devices)
    jobs = [rest_cores, mlp_out]
    key_cores = Cores(grid, *window(jobs, jobs, work, core, d_keys, normed))
    rest_out = Scatter(grid, jnp.split(rest_cores.value, [q_top + k_rows], axis=1))
    jobs = [rest_out, key_cores]
    value_cores = Cores(grid, *window([*jobs, mlp_out], jobs, work, core, d_values, normed))

    inputs_grad = None
    half = length // tile // 2
    pieces = [(s, at) for s in range(seqs) for at in (0, half)]
    for n, (s, at) in enumerate(pieces):
        if n == 0:
            starts, ends = [value_cores, rest_out], [value_cores, rest_out, mlp_out]
        elif n == 1:
            kv_out = Scatter(grid, [key_cores.value, value_cores.value])
            starts, ends = [kv_out, rest_out], [kv_out]
        elif n == 2:
            starts, ends = [kv_out], [kv_out, rest_out]
        elif n == 3:
            starts = ends = [kv_out]
        else:
            starts = ends = []
        args = (d_keys[s], d_values[s], kv_weights, g_in, byte_inputs)
        args += () if inputs_grad is None else (inputs_grad,)
        inputs_grad = window(starts, ends, functools.partial(input_grad, s, at, half), *args)
    assert not any(job.left for job in (mlp_out, rest_out, kv_out))
    both = jnp.concatenate(mlp_out.parts, axis=0)
    in_grad, back_grad = both[:q_rows], both[q_rows:]
    both = jnp.concatenate(kv_out.parts, axis=0)
    key_grad, value_grad = both[:k_rows], both[k_rows:]
    both = jnp.concatenate(rest_out.parts, axis=0)
    found = {"query": [], "out": [], "latents": []}
    for what, rows_of, columns, at, beside in unpack_rest(cuts):
        found[what].append((rows_of[0], columns[0], both[at[0] : at[1], beside[0] : beside[1]]))

    def joined(what, axis):
        pieces = sorted(found[what], key=lambda piece: piece[:2])
        return jnp.concatenate([piece[2] for piece in pieces], axis=axis)

    query_grad_mine, out_grad, base_grad = joined("query", 0), joined("out", 1), joined("latents", 1)

    def gain_grad(gain, *pairs):
        total = sum(jnp.sum(g * w.astype(F32), axis=1) for g, w in pairs)
        return total / gain.astype(F32)

    gin_grad = gain_grad(in_gain, (key_grad, key_weight), (value_grad, value_weight))
    glat_grad = gain_grad(lat_gain, (query_grad_mine, query_weight))
    gmlp_grad = gain_grad(mlp_gain, (in_grad, mlp_in_weight))
    return (
        latents,
        inputs_grad,
        base_grad,
        glat_grad,
        query_grad_mine,
        gin_grad,
        key_grad,
        value_grad,
        out_grad,
        gmlp_grad,
        in_grad,
        back_grad,
    )


def solution(mesh):
    in_specs = (
        P("dp", None, None),
        P("dp"),
        P("dp", None),
        P("dp", None, None),
        P("dp", None),
        P("dp"),
        P("dp", None),
        P("dp"),
        P("dp", None),
        P("dp", None),
        P("dp", None),
        P("dp"),
        P("dp", None),
        P("dp", None),
    )
    out_specs = (
        P("dp", None, None),
        P("dp", None, None),
        P("dp", None),
        P("dp"),
        P("dp", None),
        P("dp"),
        P("dp", None),
        P("dp", None),
        P("dp", None),
        P("dp"),
        P("dp", None),
        P("dp", None),
    )
    return jax.shard_map(local, mesh=mesh, in_specs=in_specs, out_specs=out_specs, check_vma=False)
```

```python
import functools
import math

import jax
import jax.numpy as jnp
from jax import lax
from jax.experimental import pallas as pl
from jax.experimental.pallas import tpu as pltpu
from jax.sharding import PartitionSpec as P

HEADS = 8
HEAD = 96
PADDED = 112
MASKED = -1e30
VMEM = 56 * 1024 * 1024
F32 = jnp.float32
BF16 = jnp.bfloat16


def nn(a, b):
    return lax.dot_general(a, b, (((1,), (0,)), ((), ())), preferred_element_type=F32)


def nt(a, b):
    return lax.dot_general(a, b, (((1,), (1,)), ((), ())), preferred_element_type=F32)


def tn(a, b):
    return lax.dot_general(a, b, (((0,), (0,)), ((), ())), preferred_element_type=F32)


def unit_rows(rows):
    centred = rows - jnp.mean(rows, axis=-1, keepdims=True)
    inverse = lax.rsqrt(jnp.mean(centred * centred, axis=-1, keepdims=True) + 1e-05)
    return centred * inverse, inverse


def norm_back(upstream, unit, inverse, gain):
    scaled = upstream * gain
    inner = (
        scaled
        - jnp.mean(scaled, axis=-1, keepdims=True)
        - unit * jnp.mean(scaled * unit, axis=-1, keepdims=True)
    )
    return inverse * inner


def grid_of(devices):
    known = {32: (4, 2, 2), 128: (4, 4, 4)}
    chips = devices // 2
    dims = []
    while chips > 1:
        step = next(f for f in (4, 2, 3, 5, 7, chips) if chips % f == 0)
        dims.append(step)
        chips //= step
    return (*known.get(devices, dims), 2)


class Grid:
    def __init__(self, devices):
        self.devices = devices
        self.dims = grid_of(devices)
        self.strides = tuple(math.prod(self.dims[i + 1 :]) for i in range(len(self.dims)))
        me = lax.axis_index("dp")
        self.mine = tuple((me // s) % k for s, k in zip(self.strides, self.dims))
        self.core = self.mine[-1].astype(jnp.int32).reshape(1)
        near = list(range(1, len(self.dims) - 1))
        self.order_a = (0, *near[::-1])
        self.order_b = (0, *near)

    def shift(self, dim, r):
        k, s = self.dims[dim], self.strides[dim]
        pairs = []
        for i in range(self.devices):
            at = (i // s) % k
            pairs.append((i, i + (((at + r) % k) - at) * s))
        return pairs

    def send(self, array, dim, r):
        return lax.ppermute(array, "dp", self.shift(dim, r))

    def swap(self, array, dim):
        k, s = self.dims[dim], self.strides[dim]
        firsts = [i for i in range(self.devices) if (i // s) % k == 0]
        groups = [[i + n * s for n in range(k)] for i in firsts]
        return lax.all_to_all(array, "dp", 0, 0, axis_index_groups=groups)

    def found(self, order):
        dims = self.dims[:-1]
        sizes = [dims[dim] for dim in order]
        index = jnp.zeros((1,) * len(dims), jnp.int32)
        for n, dim in enumerate(order):
            step = math.prod(sizes[:n])
            away = (jnp.arange(dims[dim], dtype=jnp.int32) - self.mine[dim]) % dims[dim]
            shape = [1] * len(dims)
            shape[dim] = dims[dim]
            index = index + (away * step).reshape(shape)
        return index.reshape(-1)


class Gather:
    def __init__(self, grid, block, cut):
        self.grid, self.cut, self.parts = grid, cut, [block[None]]
        last = len(grid.dims) - 1
        self.left = [*zip(grid.order_a, grid.order_b), (last, last)]

    def sends(self):
        one, other = self.dims = self.left.pop(0)
        if one == other:
            self.parts = [jnp.concatenate(self.parts, axis=1)] if len(self.parts) == 2 else self.parts
        elif len(self.parts) == 1:
            self.parts = jnp.split(self.parts[0], [self.cut], axis=1)
        return self.parts

    def exchange(self, sent):
        sizes = self.grid.dims
        return [
            [part] + [self.grid.send(part, dim, -r) for r in range(1, sizes[dim])]
            for dim, part in zip(self.dims, sent)
        ]

    def receive(self, got):
        self.parts = [jnp.concatenate(part, axis=0) for part in got] if self.left else got[0]


class Cores:
    def __init__(self, grid, kept, sent):
        self.grid, self.value, self.left = grid, [kept, sent], [True]

    def sends(self):
        self.left.pop()
        return self.value

    def exchange(self, sent):
        return [sent[0], self.grid.send(sent[1], len(self.grid.dims) - 1, 1)]

    def receive(self, got):
        self.value = (got[0].astype(F32) + got[1].astype(F32)).astype(got[0].dtype)


class Scatter:
    def __init__(self, grid, parts):
        self.grid = grid
        self.parts = [part.reshape(*grid.dims[:-1], *part.shape[1:]) for part in parts]
        self.left = [*zip(grid.order_a, grid.order_b)][::-1]
        self.rest = [list(range(len(grid.dims) - 1)) for _ in parts]

    def sends(self):
        self.dims = self.left.pop(0)
        if not self.left and len(self.parts) == 2:
            self.parts = [jnp.concatenate(self.parts, axis=1)]
        if not self.left:
            return self.parts
        sent = []
        for part, dim, rest in zip(self.parts, self.dims, self.rest):
            axis, k, me = rest.index(dim), self.grid.dims[dim], self.grid.mine[dim]
            rest.remove(dim)
            sent.append(
                [lax.dynamic_index_in_dim(part, (me + r) % k, axis, keepdims=False) for r in range(k)]
            )
        return sent

    def exchange(self, sent):
        if not self.left:
            return [self.grid.swap(part, self.dims[0]) for part in sent]
        return [
            part[:1] + [self.grid.send(piece, dim, r) for r, piece in enumerate(part) if r]
            for dim, part in zip(self.dims, sent)
        ]

    def receive(self, got):
        if not self.left:
            self.parts = [jnp.sum(part.astype(F32), axis=0) for part in got]
            return
        totals = [sum(piece.astype(F32) for piece in part) for part in got]
        self.parts = [total.astype(got[0][0].dtype) for total in totals]


def window(starts, ends, work=None, *args):
    sent, args = lax.optimization_barrier(([job.sends() for job in starts], args))
    for job, parts in zip(starts, sent):
        job.running = job.exchange(parts)
    out = work(*args) if work else ()
    got, out = lax.optimization_barrier(([job.running for job in ends], out))
    for job, parts in zip(ends, got):
        job.receive(parts)
    return out


def by_core(core_ref, one, other):
    first = core_ref[0] == 0
    return jnp.where(first, one, other), jnp.where(first, other, one)


def pack_kernel(
    gains_ref, key_ref, value_ref, query_ref, lat_ref, out_ref, in_ref, back_ref, one_ref, two_ref, three_ref
):
    k_rows, width = key_ref.shape
    q_rows, (l_rows, l_width) = query_ref.shape[0], lat_ref.shape
    one_ref[:k_rows] = key_ref[...]
    one_ref[k_rows : 2 * k_rows] = value_ref[...]
    one_ref[2 * k_rows :] = gains_ref[...]
    two_ref[:q_rows] = query_ref[...]
    two_ref[q_rows : q_rows + l_rows] = lat_ref[:, :width]
    tail = jnp.concatenate([lat_ref[:, width:], jnp.zeros((l_rows, 2 * width - l_width), BF16)], axis=1)
    two_ref[q_rows + l_rows :] = tail
    three_ref[:, :l_width] = in_ref[...]
    three_ref[:, l_width : 2 * l_width] = back_ref[...]
    size = k_rows // 3
    side = jnp.concatenate([out_ref[n * size : (n + 1) * size] for n in range(3)], axis=1)
    piece = three_ref.shape[1] - 2 * l_width
    for n in range(side.shape[1] // piece):
        three_ref[n * size : (n + 1) * size, 2 * l_width :] = side[:, n * piece : (n + 1) * piece]


def pack(gains, key, value, query, latents, out, w_in, w_back):
    k_rows, width = key.shape
    q_rows, (l_rows, l_width) = query.shape[0], latents.shape
    vmem = pl.BlockSpec(memory_space=pltpu.VMEM)
    shapes = [
        (2 * k_rows + gains.shape[0], width),
        (q_rows + 2 * l_rows, width),
        (q_rows, 2 * l_width + k_rows * l_width // q_rows),
    ]
    return pl.pallas_call(
        pack_kernel,
        in_specs=[vmem] * 8,
        out_specs=[vmem] * 3,
        out_shape=[jax.ShapeDtypeStruct(s, BF16) for s in shapes],
        cost_estimate=pl.CostEstimate(flops=0, bytes_accessed=1_000_000, transcendentals=0),
        name="pack",
    )(gains, key, value, query, latents, out, w_in, w_back)


def prepare_kv_kernel(cuts, core_ref, place_ref, own_ref, other_ref, wt_ref, gin_ref, glat_ref, gmlp_ref, kv_ref):
    chips, _, width = own_ref.shape
    k_rows = width // (2 * chips)
    lines = []
    for chip in range(chips):
        at = [place_ref[n, chip] for n in range(2)]
        keys = by_core(core_ref, own_ref[at[0], :k_rows], other_ref[at[0], :k_rows])
        values = by_core(core_ref, own_ref[at[1], k_rows : 2 * k_rows], other_ref[at[1], k_rows : 2 * k_rows])
        both = by_core(core_ref, own_ref[at[1], 2 * k_rows :], other_ref[at[1], 2 * k_rows :])
        for n in range(2):
            mine = slice((2 * chip + n) * k_rows, (2 * chip + n + 1) * k_rows)
            kv_ref[mine, :width] = keys[n]
            kv_ref[mine, width:] = values[n]
            lines.append(both[n][:1].astype(F32))
    first = 0
    for ref, size in zip((gin_ref, glat_ref, gmlp_ref), cuts):
        ref[...] = jnp.concatenate([line[:, first : first + size] for line in lines], axis=1)
        first += size
    for c in range(0, wt_ref.shape[0], width):
        wt_ref[c : c + width] = kv_ref[:, c : c + width].T


def prepare_kv(core, places, stacks, cuts):
    width = stacks[0].shape[-1]
    devices = 2 * stacks[0].shape[0]
    vmem = pl.BlockSpec(memory_space=pltpu.VMEM)
    smem = pl.BlockSpec(memory_space=pltpu.SMEM)
    shapes = [((2 * width, width), BF16)] + [((1, devices * size), F32) for size in cuts]
    return pl.pallas_call(
        functools.partial(prepare_kv_kernel, cuts),
        in_specs=[smem, smem, vmem, vmem],
        out_specs=[vmem] * len(shapes),
        out_shape=[jax.ShapeDtypeStruct(*s) for s in shapes],
        scratch_shapes=[pltpu.VMEM((width, 2 * width), BF16)],
        compiler_params=pltpu.CompilerParams(vmem_limit_bytes=VMEM),
        cost_estimate=pl.CostEstimate(flops=0, bytes_accessed=12_000_000, transcendentals=0),
        name="prepare_kv",
    )(core, places, *stacks)


def unpack_rest(cuts):
    q_top, q_low, k_rows, l_rows, width, l_width = cuts
    spare = 2 * width - l_width
    second = q_top + k_rows
    third = second + k_rows
    found = [
        ("query", (0, q_top), (0, width), (0, q_top), (0, width)),
        ("out", (0, k_rows), (0, width), (q_top, second), (0, width)),
        ("out", (0, k_rows), (width, l_width), (second, third), (0, l_width - width)),
        ("query", (q_top, q_top + q_low), (0, width), (third, third + q_low), (0, width)),
        ("latents", (0, l_rows), (0, width), (third + q_low, third + q_low + l_rows), (0, width)),
    ]
    for n, at in enumerate(range(width, l_width, spare)):
        end = min(at + spare, l_width)
        start = second + n * l_rows
        found.append(
            ("latents", (0, l_rows), (at, end), (start, start + l_rows), (l_width - width, l_width - width + end - at))
        )
    return found


def prepare_q_kernel(cuts, core_ref, place_ref, own_ref, other_ref, glat_ref, wq_ref, lat_ref, q_ref, qt_ref):
    chips, _, width = own_ref.shape
    q_top, q_low, _, l_rows, _, l_width = cuts
    q_rows = q_top + q_low
    head = q_rows + l_rows
    pieces = [
        (0, wq_ref, q_rows, (0, q_top), (0, width), 0),
        (1, wq_ref, q_rows, (q_top, q_rows), (0, width), q_top),
        (1, lat_ref, l_rows, (q_rows, head), (0, width), 0),
        (1, lat_ref, l_rows, (head, head + l_rows), (width, l_width), 0),
    ]
    for chip in range(chips):
        for part, ref, size, (first, last), (left, right), row in pieces:
            place = place_ref[part, chip]
            span = slice(0, right - left)
            both = by_core(core_ref, own_ref[place, first:last, span], other_ref[place, first:last, span])
            for n in range(2):
                base = (2 * chip + n) * size + row
                ref[base : base + last - first, left:right] = both[n]
    unit, _ = unit_rows(lat_ref[...].astype(F32))
    query = nn((unit * glat_ref[...]).astype(BF16), wq_ref[...])
    qt_ref[...] = query.T.astype(BF16)
    query = query.astype(BF16)
    column = lax.broadcasted_iota(jnp.int32, (query.shape[0], PADDED - HEAD), 1)
    ones = jnp.where(column == 0, 1.0, 0.0).astype(BF16)
    for h in range(HEADS):
        q_ref[h] = jnp.concatenate([query[:, h * HEAD : (h + 1) * HEAD], ones], axis=1)


def prepare_q(core, places, stacks, gain, cuts):
    devices = 2 * stacks[0].shape[0]
    q_top, q_low, _, l_rows, width, l_width = cuts
    rows = devices * l_rows
    vmem = pl.BlockSpec(memory_space=pltpu.VMEM)
    smem = pl.BlockSpec(memory_space=pltpu.SMEM)
    shapes = [(devices * (q_top + q_low), width), (rows, l_width), (HEADS, rows, PADDED), (width, rows)]
    return pl.pallas_call(
        functools.partial(prepare_q_kernel, cuts),
        in_specs=[smem, smem, vmem, vmem, vmem],
        out_specs=[vmem] * len(shapes),
        out_shape=[jax.ShapeDtypeStruct(s, BF16) for s in shapes],
        compiler_params=pltpu.CompilerParams(vmem_limit_bytes=VMEM),
        cost_estimate=pl.CostEstimate(flops=0, bytes_accessed=12_000_000, transcendentals=0),
        name="prepare_q",
    )(core, places, *stacks, gain)


def project_kernel(x_ref, gain_ref, w_ref, addend_ref, *refs):
    normed_ref, k_ref, v_ref = refs[-3:]
    unit, _ = unit_rows(x_ref[0].astype(F32))
    normed = (unit * gain_ref[...]).astype(BF16)
    normed_ref[0] = normed
    slots = normed.shape[0]
    both = nt(w_ref[...], normed).astype(BF16)
    row = lax.broadcasted_iota(jnp.int32, (PADDED - HEAD, slots), 0)
    mask_rows = jnp.where(row == 0, jnp.broadcast_to(addend_ref[0], row.shape), 0.0).astype(BF16)
    one_rows = jnp.where(row < 3, 1.0, 0.0).astype(BF16)
    for h in range(HEADS):
        k_ref[0, h, :HEAD] = both[h * HEAD : (h + 1) * HEAD]
        k_ref[0, h, HEAD:] = mask_rows
        v_ref[0, h, :HEAD] = both[(HEADS + h) * HEAD : (HEADS + h + 1) * HEAD]
        v_ref[0, h, HEAD:] = one_rows


def project(first, steps, tile, x, gain, weights, addend, *into):
    seqs, slots, width = x.shape
    tiles = slots // tile
    at = lambda i: ((first + i) // tiles, (first + i) % tiles)
    rows = pl.BlockSpec((1, tile, width), lambda i: (*at(i), 0))
    heads = pl.BlockSpec((1, HEADS, PADDED, tile), lambda i: (at(i)[0], 0, 0, at(i)[1]))
    whole = lambda a: pl.BlockSpec(a.shape, lambda i: (0,) * a.ndim)
    mask = pl.BlockSpec((1, 1, tile), lambda i: (at(i)[0], 0, at(i)[1]))
    return pl.pallas_call(
        project_kernel,
        grid=(steps,),
        in_specs=[rows, whole(gain), whole(weights), mask] + [pl.BlockSpec(memory_space=pl.ANY)] * len(into),
        out_specs=[rows, heads, heads],
        out_shape=[
            jax.ShapeDtypeStruct((seqs, slots, width), BF16),
            jax.ShapeDtypeStruct((seqs, HEADS, PADDED, slots), BF16),
            jax.ShapeDtypeStruct((seqs, HEADS, PADDED, slots), BF16),
        ],
        input_output_aliases={4 + n: n for n in range(len(into))},
        compiler_params=pltpu.CompilerParams(vmem_limit_bytes=VMEM),
        cost_estimate=pl.CostEstimate(
            flops=8 * steps * tile * width * width, bytes_accessed=10 * steps * tile * width, transcendentals=0
        ),
        name="project",
    )(x, gain, weights, addend, *into)


def attend_kernel(chunk, scale, q_ref, k_ref, v_ref, mixed_ref, power_ref, weight_ref, score_ref):
    slots = k_ref.shape[-1]
    outs = []
    lane = lax.broadcasted_iota(jnp.int32, weight_ref.shape[2:], 1)
    weights = jnp.zeros(lane.shape, F32)
    for h in range(q_ref.shape[0]):
        score = score_ref.at[h % 2]
        top = None
        for j in range(0, slots, chunk):
            piece = nn(q_ref[h], k_ref[0, h, :, j : j + chunk])
            score[:, j : j + chunk] = piece
            for t in range(0, chunk, 128):
                part = piece[:, t : t + 128]
                top = part if top is None else jnp.maximum(top, part)
        top = jnp.max(top, axis=-1, keepdims=True)
        total = None
        for j in range(0, slots, chunk):
            power = jnp.exp2((score[:, j : j + chunk] - top) * scale).astype(BF16)
            power_ref[0, h, :, j : j + chunk] = power
            piece = nt(power, v_ref[0, h, :, j : j + chunk])
            total = piece if total is None else total + piece
        weight = 1.0 / total[:, HEAD : HEAD + 1]
        outs.append(total[:, :HEAD] * weight)
        weights = jnp.where(lane == h, weight, weights)
    mixed_ref[0, 0] = jnp.concatenate(outs, axis=1)
    weight_ref[0, 0] = weights


def attend(q, k, v, chunk=1024, group=4):
    seqs, slots, rows = k.shape[0], k.shape[-1], q.shape[1]
    scale = math.log2(math.e) / math.sqrt(HEAD)
    heads = pl.BlockSpec((1, group, PADDED, slots), lambda s, g: (s, g, 0, 0))
    return pl.pallas_call(
        functools.partial(attend_kernel, chunk, scale),
        grid=(seqs, HEADS // group),
        in_specs=[pl.BlockSpec((group, rows, PADDED), lambda s, g: (g, 0, 0)), heads, heads],
        out_specs=[
            pl.BlockSpec((1, 1, rows, group * HEAD), lambda s, g: (s, g, 0, 0)),
            pl.BlockSpec((1, group, rows, slots), lambda s, g: (s, g, 0, 0)),
            pl.BlockSpec((1, 1, rows, 128), lambda s, g: (s, g, 0, 0)),
        ],
        out_shape=[
            jax.ShapeDtypeStruct((seqs, HEADS // group, rows, group * HEAD), F32),
            jax.ShapeDtypeStruct((seqs, HEADS, rows, slots), BF16),
            jax.ShapeDtypeStruct((seqs, HEADS // group, rows, 128), F32),
        ],
        scratch_shapes=[pltpu.VMEM((2, rows, slots), F32)],
        compiler_params=pltpu.CompilerParams(vmem_limit_bytes=VMEM),
        cost_estimate=pl.CostEstimate(
            flops=16 * seqs * rows * slots * HEADS * HEAD,
            bytes_accessed=4 * seqs * HEADS * PADDED * slots,
            transcendentals=seqs * HEADS * rows * slots,
        ),
        name="attend",
    )(q, k, v)


def attend_back_kernel(factor, qt_ref, k_ref, v_ref, power_ref, dm_ref, dmt_ref, dq_ref, dk_ref, dv_ref):
    grads = []
    for h in range(power_ref.shape[1]):
        mine = slice(h * HEAD, (h + 1) * HEAD)
        power = power_ref[0, h]
        d_scores = (power.astype(F32) * nn(dm_ref[0, h], v_ref[0, h])).astype(BF16)
        dv_ref[0, mine] = nn(dmt_ref[0, mine], power).astype(BF16)
        dk_ref[0, mine] = (nn(qt_ref[mine], d_scores) * factor).astype(BF16)
        grads.append((nt(d_scores, k_ref[0, h, :HEAD]) * factor).astype(BF16))
    dq_ref[0] = jnp.concatenate(grads, axis=1)


def attend_back(seq, qt, k, v, power, dm, dmt, group=4):
    slots, rows = k.shape[-1], qt.shape[1]
    heads = pl.BlockSpec((1, group, PADDED, slots), lambda g: (seq, g, 0, 0))
    features = pl.BlockSpec((1, group * HEAD, slots), lambda g: (0, g, 0))
    return pl.pallas_call(
        functools.partial(attend_back_kernel, 1.0 / math.sqrt(HEAD)),
        grid=(HEADS // group,),
        in_specs=[
            pl.BlockSpec((group * HEAD, rows), lambda g: (g, 0)),
            heads,
            heads,
            pl.BlockSpec((1, group, rows, slots), lambda g: (seq, g, 0, 0)),
            pl.BlockSpec((1, group, rows, PADDED), lambda g: (seq, g, 0, 0)),
            pl.BlockSpec((1, group * HEAD, rows), lambda g: (seq, g, 0)),
        ],
        out_specs=[pl.BlockSpec((1, rows, group * HEAD), lambda g: (g, 0, 0)), features, features],
        out_shape=[
            jax.ShapeDtypeStruct((HEADS // group, rows, group * HEAD), BF16),
            jax.ShapeDtypeStruct((1, HEADS * HEAD, slots), BF16),
            jax.ShapeDtypeStruct((1, HEADS * HEAD, slots), BF16),
        ],
        compiler_params=pltpu.CompilerParams(vmem_limit_bytes=VMEM),
        cost_estimate=pl.CostEstimate(
            flops=32 * rows * slots * HEADS * HEAD,
            bytes_accessed=8 * HEADS * PADDED * slots + 2 * HEADS * rows * slots,
            transcendentals=0,
        ),
        name="attend_back",
    )(qt, k, v, power, dm, dmt)


def weight_grad_kernel(seqs, core_ref, *refs):
    grads, normed_ref, (kept_ref, sent_ref, total_ref) = refs[:seqs], refs[seqs], refs[seqs + 1 :]
    chips, rows, _ = kept_ref.shape
    piece = sum(nn(grad[0], normed_ref[s]) for s, grad in enumerate(grads))

    @pl.when(pl.program_id(0) == 0)
    def _():
        total_ref[...] = piece

    @pl.when(pl.program_id(0) > 0)
    def _():
        total_ref[...] += piece

    @pl.when(pl.program_id(0) == pl.num_programs(0) - 1)
    def _():
        whole = total_ref[...].T
        for chip in range(chips):
            at = 2 * chip * rows
            kept, sent = by_core(core_ref, whole[at : at + rows], whole[at + rows : at + 2 * rows])
            kept_ref[chip] = kept.astype(BF16)
            sent_ref[chip] = sent.astype(BF16)


def weight_grad(core, grads, normed, devices, tile=1024):
    seqs, slots, width = normed.shape
    features = grads[0].shape[1]
    columns = pl.BlockSpec((1, features, tile), lambda j: (0, 0, j))
    shape = (devices // 2, width // devices, features)
    return pl.pallas_call(
        functools.partial(weight_grad_kernel, seqs),
        grid=(slots // tile,),
        in_specs=[pl.BlockSpec(memory_space=pltpu.SMEM)]
        + [columns] * seqs
        + [pl.BlockSpec((seqs, tile, width), lambda j: (0, j, 0))],
        out_specs=[pl.BlockSpec(shape, lambda j: (0, 0, 0))] * 2,
        out_shape=[jax.ShapeDtypeStruct(shape, BF16)] * 2,
        scratch_shapes=[pltpu.VMEM((features, width), F32)],
        compiler_params=pltpu.CompilerParams(vmem_limit_bytes=VMEM),
        cost_estimate=pl.CostEstimate(
            flops=4 * seqs * slots * width * features, bytes_accessed=4 * seqs * slots * width, transcendentals=0
        ),
        name="weight_grad",
    )(core, *grads, normed)


def query_grad_kernel(seqs, cuts, core_ref, *refs):
    grads, (base_ref, gain_ref, wq_ref, rest_ref, go_ref, kept_ref, sent_ref) = refs[:seqs], refs[seqs:]
    chips = kept_ref.shape[0]
    unit, inverse = unit_rows(base_ref[...].astype(F32))
    normed = (unit * gain_ref[...]).astype(BF16)
    grads = [jnp.concatenate([grad[g] for g in range(grad.shape[0])], axis=1) for grad in grads]
    query = sum(tn(normed, grad) for grad in grads)
    back = sum(nt(grad, wq_ref[...]) for grad in grads)
    latents = norm_back(back, unit, inverse, gain_ref[...]) + rest_ref[...]
    wholes = {"query": query, "out": go_ref[...].astype(F32), "latents": latents}
    for chip in range(chips):
        for what, rows, columns, at, beside in unpack_rest(cuts):
            whole = wholes[what]
            size = whole.shape[0] // (2 * chips)
            pieces = [
                whole[base + rows[0] : base + rows[1], columns[0] : columns[1]]
                for base in (2 * chip * size, (2 * chip + 1) * size)
            ]
            for ref, piece in zip((kept_ref, sent_ref), by_core(core_ref, *pieces)):
                ref[chip, at[0] : at[1], beside[0] : beside[1]] = piece.astype(BF16)


def query_grad(core, grads, base, gain, w_query, rest, grad_out, devices, cuts):
    q_top, q_low, k_rows, l_rows, width, l_width = cuts
    vmem = pl.BlockSpec(memory_space=pltpu.VMEM)
    shape = (devices // 2, q_top + q_low + 2 * k_rows + l_rows, width)
    return pl.pallas_call(
        functools.partial(query_grad_kernel, len(grads), cuts),
        in_specs=[pl.BlockSpec(memory_space=pltpu.SMEM)] + [vmem] * (len(grads) + 5),
        out_specs=[vmem] * 2,
        out_shape=[jax.ShapeDtypeStruct(shape, BF16)] * 2,
        compiler_params=pltpu.CompilerParams(vmem_limit_bytes=VMEM),
        cost_estimate=pl.CostEstimate(
            flops=4 * len(grads) * base.shape[0] * l_width * width, bytes_accessed=12_000_000, transcendentals=0
        ),
        name="query_grad",
    )(core, *grads, base, gain, w_query, rest, grad_out)


def input_grad_kernel(dk_ref, dv_ref, w_ref, gain_ref, x_ref, *refs):
    out_ref = refs[-1]
    features = dk_ref.shape[1]
    upstream = tn(dk_ref[0], w_ref[:features]) + tn(dv_ref[0], w_ref[features:])
    unit, inverse = unit_rows(x_ref[0].astype(F32))
    out_ref[0] = norm_back(upstream, unit, inverse, gain_ref[...]).astype(BF16)


def input_grad(seq, first, steps, dk, dv, weights, gain, x, into=None, tile=512):
    features = dk.shape[1]
    width = x.shape[-1]
    columns = pl.BlockSpec((1, features, tile), lambda j: (0, 0, first + j))
    rows = pl.BlockSpec((1, tile, width), lambda j: (seq, first + j, 0))
    whole = lambda a: pl.BlockSpec(a.shape, lambda j: (0,) * a.ndim)
    args = [dk, dv, weights, gain, x] + ([] if into is None else [into])
    specs = [columns, columns, whole(weights), whole(gain), rows]
    return pl.pallas_call(
        input_grad_kernel,
        grid=(steps,),
        in_specs=specs + [pl.BlockSpec(memory_space=pl.ANY)] * (len(args) - len(specs)),
        out_specs=rows,
        out_shape=jax.ShapeDtypeStruct(x.shape, BF16),
        input_output_aliases={} if into is None else {5: 0},
        compiler_params=pltpu.CompilerParams(vmem_limit_bytes=VMEM),
        cost_estimate=pl.CostEstimate(
            flops=8 * steps * tile * width * features, bytes_accessed=8 * steps * tile * width, transcendentals=0
        ),
        name="input_grad",
    )(*args)


def gelu_parts(pre):
    cdf = 0.5 * (1.0 + lax.erf(pre * (1.0 / math.sqrt(2.0))))
    slope = cdf + pre * jnp.exp(-0.5 * pre * pre) * (1.0 / math.sqrt(2.0 * math.pi))
    return pre * cdf, slope


def feed_forward_kernel(
    core_ref, mixed_ref, weight_ref, base_ref, late_ref, gain_ref, cot_ref,
    latents_out, kept_out, sent_out, g_out_out, rest_out, dm_ref, dmt_ref,
    w_in_ref, w_back_ref, side_ref, w_out_ref, mlp_ref, act_ref, pre_ref, attn_ref, mix_ref,
    latents_ref, kept_ref, sent_ref, g_out_ref, rest_ref, come, go,
):
    seqs, groups, rows, columns = mixed_ref.shape
    width, l_width = groups * columns, base_ref.shape[1]
    arrivals = [
        pltpu.make_async_copy(late_ref.at[:, first : first + ref.shape[1]], ref, come.at[n])
        for n, (ref, first) in enumerate(((side_ref, 2 * l_width), (w_in_ref, 0), (w_back_ref, l_width)))
    ]
    for copy in arrivals:
        copy.start()
    pairs = [
        (latents_ref, latents_out), (rest_ref, rest_out), (kept_ref, kept_out), (sent_ref, sent_out), (g_out_ref, g_out_out)
    ]
    leaves = [pltpu.make_async_copy(ref, out, go.at[n]) for n, (ref, out) in enumerate(pairs)]

    gain = gain_ref[...]
    base = base_ref[...].astype(F32)
    for s in range(seqs):
        whole = jnp.concatenate([mixed_ref[s, g] for g in range(groups)], axis=1)
        mix_ref[s * rows : (s + 1) * rows] = whole.astype(BF16)
    arrivals[0].wait()
    chips = kept_ref.shape[0]
    devices = 2 * chips
    u = width // devices // 3
    part = side_ref.shape[1]
    for d in range(devices):
        for n in range(3 * l_width // part):
            block = side_ref[(d * (side_ref.shape[0] // devices)) + n * u : d * (side_ref.shape[0] // devices) + (n + 1) * u]
            at = n * part
            while at < (n + 1) * part:
                row, left = divmod(at, l_width)
                size = min(l_width - left, (n + 1) * part - at)
                base_row = 3 * u * d + row * u
                w_out_ref[base_row : base_row + u, left : left + size] = block[:, at - n * part : at - n * part + size]
                at += size
    norms, ones, bars = [], [], []
    for s in range(seqs):
        mine = slice(s * rows, (s + 1) * rows)
        x_one = base + nn(mix_ref[mine], w_out_ref[...])
        unit, inverse = unit_rows(x_one)
        mlp_ref[mine] = (unit * gain).astype(BF16)
        norms.append((unit, inverse))
        ones.append(x_one)
    arrivals[1].wait()
    arrivals[2].wait()
    for s in range(seqs):
        mine = slice(s * rows, (s + 1) * rows)
        pre = nn(mlp_ref[mine], w_in_ref[...])
        value, slope = gelu_parts(pre)
        act_ref[mine] = value.astype(BF16)
        pre_ref[mine] = (nt(cot_ref[s], w_back_ref[...]) * slope).astype(BF16)
    for s in range(seqs):
        mine = slice(s * rows, (s + 1) * rows)
        latents_ref[s] = (ones[s] + nn(act_ref[mine], w_back_ref[...])).astype(BF16)
        back = nt(pre_ref[mine], w_in_ref[...])
        bar = cot_ref[s].astype(F32) + norm_back(back, *norms[s], gain)
        attn_ref[mine] = bar.astype(BF16)
        bars.append(bar)
    rest_ref[...] = sum(bars)
    leaves[0].start()
    leaves[1].start()
    cot = jnp.concatenate([cot_ref[s] for s in range(seqs)], axis=0)
    size = l_width // devices
    for n, whole in enumerate((tn(mlp_ref[...], pre_ref[...]), tn(act_ref[...], cot))):
        for chip in range(chips):
            at = 2 * chip * size
            both = by_core(core_ref, whole[at : at + size], whole[at + size : at + 2 * size])
            for ref, block in zip((kept_ref, sent_ref), both):
                ref[chip, n * size : (n + 1) * size] = block.astype(BF16)
    leaves[2].start()
    leaves[3].start()
    g_out_ref[...] = tn(mix_ref[...], attn_ref[...]).astype(BF16)
    leaves[4].start()
    column = lax.broadcasted_iota(jnp.int32, (rows, PADDED - HEAD), 1)
    group = HEADS // weight_ref.shape[1]
    for s in range(seqs):
        mine = slice(s * rows, (s + 1) * rows)
        d_mixed = nt(attn_ref[mine], w_out_ref[...])
        parts = []
        for h in range(HEADS):
            weight = weight_ref[s, h // group, :, h % group : h % group + 1]
            parts.append(d_mixed[:, h * HEAD : (h + 1) * HEAD] * weight)
        dmt_ref[s] = jnp.concatenate(parts, axis=1).T.astype(BF16)
        for h, part in enumerate(parts):
            part = part.astype(BF16)
            head = h % group * HEAD
            mixed = mixed_ref[s, h // group, :, head : head + HEAD]
            centre = -jnp.sum(part.astype(F32) * mixed, axis=-1, keepdims=True)
            high = centre.astype(BF16).astype(F32)
            middle = (centre - high).astype(BF16).astype(F32)
            low = centre - high - middle
            pieces = jnp.where(column == 0, high, jnp.where(column == 1, middle, jnp.where(column == 2, low, 0.0)))
            dm_ref[s, h] = jnp.concatenate([part, pieces.astype(BF16)], axis=1)
    for copy in leaves:
        copy.wait()


def feed_forward(core, mixed, weight, base, late, gain, cot, devices):
    seqs, groups, rows, columns = mixed.shape
    width, l_width = groups * columns, base.shape[1]
    vmem = pl.BlockSpec(memory_space=pltpu.VMEM)
    anywhere = pl.BlockSpec(memory_space=pl.ANY)
    blocks = ((devices // 2, 2 * (l_width // devices), l_width), BF16)
    moved = [(cot.shape, BF16), blocks, blocks, ((width, l_width), BF16), (base.shape, F32)]
    shapes = moved + [((seqs, HEADS, rows, PADDED), BF16), ((seqs, width, rows), BF16)]
    many = seqs * rows
    square = pltpu.VMEM((l_width, l_width), BF16)
    return pl.pallas_call(
        feed_forward_kernel,
        in_specs=[pl.BlockSpec(memory_space=pltpu.SMEM), vmem, vmem, vmem, anywhere, vmem, vmem],
        out_specs=[anywhere] * len(moved) + [vmem] * 2,
        out_shape=[jax.ShapeDtypeStruct(*s) for s in shapes],
        scratch_shapes=[
            square,
            square,
            pltpu.VMEM((l_width, late.shape[1] - 2 * l_width), BF16),
            pltpu.VMEM((width, l_width), BF16),
            *[pltpu.VMEM((many, l_width), BF16)] * 4,
            pltpu.VMEM((many, width), BF16),
            *[pltpu.VMEM(*s) for s in moved],
            pltpu.SemaphoreType.DMA((3,)),
            pltpu.SemaphoreType.DMA((len(moved),)),
        ],
        compiler_params=pltpu.CompilerParams(vmem_limit_bytes=VMEM),
        cost_estimate=pl.CostEstimate(
            flops=6 * many * l_width * (width + 2 * l_width), bytes_accessed=24_000_000, transcendentals=0
        ),
        name="feed_forward",
    )(core, mixed, weight, base, late, gain, cot)


def local(
    byte_inputs,
    lengths,
    key_mask,
    latents_cot,
    latent_array,
    lat_gain,
    query_weight,
    in_gain,
    key_weight,
    value_weight,
    out_weight,
    mlp_gain,
    mlp_in_weight,
    mlp_out_weight,
):
    devices = lax.axis_size("dp")
    grid = Grid(devices)
    seqs, length, width = byte_inputs.shape
    k_rows, q_rows, l_rows = key_weight.shape[0], query_weight.shape[0], latent_array.shape[0]
    l_width = latent_array.shape[1]
    q_top = k_rows if q_rows > k_rows else q_rows // 2
    q_low = q_rows - q_top

    gains = jnp.concatenate([in_gain, lat_gain, mlp_gain])
    sizes = (in_gain.shape[0], lat_gain.shape[0], mlp_gain.shape[0])
    gain_rows = jnp.broadcast_to(jnp.pad(gains, (0, width - gains.shape[0])), (8, width))
    one, two, three = pack(
        gain_rows, key_weight, value_weight, query_weight, latent_array, out_weight, mlp_in_weight, mlp_out_weight
    )
    first = Gather(grid, one, k_rows)
    second = Gather(grid, two, q_top)
    late = lax.all_gather(three, "dp", axis=0, tiled=True)
    cuts = (q_top, q_low, k_rows, l_rows, width, l_width)
    window([first], [first])
    positions = jnp.arange(length, dtype=jnp.int32)
    valid = (positions[None, :] < lengths[:, None]) & (key_mask == 1)
    addend = jnp.where(valid, 0.0, MASKED).astype(F32)[:, None]
    places = jnp.stack([grid.found(grid.order_a), grid.found(grid.order_b)])
    while len(first.left) > 2:
        addend, places = window([first], [first], lambda *early: early, addend, places)
    window([first, second], [first, second])
    window([first, second], [first])
    core = grid.core
    kv_weights, g_in, g_lat, g_mlp = window(
        [], [second], functools.partial(prepare_kv, cuts=sizes), core, places, first.parts
    )
    tile = 512
    tiles = seqs * (length // tile)
    lag = max(tiles // 4, 1)
    given = (byte_inputs, g_in, kv_weights, addend)
    while len(second.left) > 1:
        made = window([second], [second], functools.partial(project, 0, tiles - lag, tile), *given)
    normed, k, v = window(
        [second], [second], functools.partial(project, tiles - lag, lag, tile), *given, *made
    )
    w_query, base, q, qt = prepare_q(core, places, second.parts, g_lat, cuts)
    mixed, power, weight = attend(q, k, v)
    latents, kept, sent, grad_out, rest, dm, dmt = feed_forward(
        core, mixed, weight, base, late, g_mlp, latents_cot, devices
    )

    mlp_cores = Cores(grid, kept, sent)
    given = (qt, k, v, power, dm, dmt)
    backs = [window([mlp_cores], [mlp_cores], functools.partial(attend_back, 0), *given)]
    mlp_out = Scatter(grid, jnp.split(mlp_cores.value, [q_rows], axis=1))
    for s in range(1, seqs):
        backs.append(window([mlp_out] if s == 1 else [], [], functools.partial(attend_back, s), *given))
    d_query, d_keys, d_values = zip(*backs)
    work = functools.partial(query_grad, devices=devices, cuts=cuts)
    rest_cores = Cores(
        grid, *window([], [mlp_out], work, core, d_query, base, g_lat, w_query, rest, grad_out)
    )
    work = functools.partial(weight_grad, devices=devices)
    jobs = [rest_cores, mlp_out]
    key_cores = Cores(grid, *window(jobs, jobs, work, core, d_keys, normed))
    rest_out = Scatter(grid, jnp.split(rest_cores.value, [q_top + k_rows], axis=1))
    jobs = [rest_out, key_cores]
    value_cores = Cores(grid, *window([*jobs, mlp_out], jobs, work, core, d_values, normed))

    inputs_grad = None
    half = length // tile // 2
    pieces = [(s, at) for s in range(seqs) for at in (0, half)]
    for n, (s, at) in enumerate(pieces):
        if n == 0:
            starts, ends = [value_cores, rest_out], [value_cores, rest_out, mlp_out]
        elif n == 1:
            kv_out = Scatter(grid, [jnp.concatenate([key_cores.value, value_cores.value], axis=1)])
            starts, ends = [kv_out, rest_out], [kv_out]
        elif n == 2:
            starts, ends = [kv_out], [kv_out, rest_out]
        elif n == 3:
            starts = ends = [kv_out]
        else:
            starts = ends = []
        args = (d_keys[s], d_values[s], kv_weights, g_in, byte_inputs)
        args += () if inputs_grad is None else (inputs_grad,)
        inputs_grad = window(starts, ends, functools.partial(input_grad, s, at, half), *args)
    assert not any(job.left for job in (mlp_out, rest_out, kv_out))
    both = jnp.concatenate(mlp_out.parts, axis=0)
    in_grad, back_grad = both[:q_rows], both[q_rows:]
    both = jnp.concatenate(kv_out.parts, axis=0)
    key_grad, value_grad = both[:k_rows], both[k_rows:]
    both = jnp.concatenate(rest_out.parts, axis=0)
    found = {"query": [], "out": [], "latents": []}
    for what, rows_of, columns, at, beside in unpack_rest(cuts):
        found[what].append((rows_of[0], columns[0], both[at[0] : at[1], beside[0] : beside[1]]))

    def joined(what, axis):
        pieces = sorted(found[what], key=lambda piece: piece[:2])
        return jnp.concatenate([piece[2] for piece in pieces], axis=axis)

    query_grad_mine, out_grad, base_grad = joined("query", 0), joined("out", 1), joined("latents", 1)

    def gain_grad(gain, *pairs):
        total = sum(jnp.sum(g * w.astype(F32), axis=1) for g, w in pairs)
        return total / gain.astype(F32)

    gin_grad = gain_grad(in_gain, (key_grad, key_weight), (value_grad, value_weight))
    glat_grad = gain_grad(lat_gain, (query_grad_mine, query_weight))
    gmlp_grad = gain_grad(mlp_gain, (in_grad, mlp_in_weight))
    return (
        latents,
        inputs_grad,
        base_grad,
        glat_grad,
        query_grad_mine,
        gin_grad,
        key_grad,
        value_grad,
        out_grad,
        gmlp_grad,
        in_grad,
        back_grad,
    )


def solution(mesh):
    in_specs = (
        P("dp", None, None),
        P("dp"),
        P("dp", None),
        P("dp", None, None),
        P("dp", None),
        P("dp"),
        P("dp", None),
        P("dp"),
        P("dp", None),
        P("dp", None),
        P("dp", None),
        P("dp"),
        P("dp", None),
        P("dp", None),
    )
    out_specs = (
        P("dp", None, None),
        P("dp", None, None),
        P("dp", None),
        P("dp"),
        P("dp", None),
        P("dp"),
        P("dp", None),
        P("dp", None),
        P("dp", None),
        P("dp"),
        P("dp", None),
        P("dp", None),
    )
    return jax.shard_map(local, mesh=mesh, in_specs=in_specs, out_specs=out_specs, check_vma=False)
```
